32 devices in a mesh: row: 8 (over z, x), col: 4 (over y, core).
Axes of the slice: x: 2, y: 2, z: 4, core: 2. Of those that a mesh axis runs over, the one named last changes fastest.
Arguments:
- homolog_matrix: bfloat16 [64, 320, 64], P('row', 'col'), may hold values from -6 to 6
- contact_matrix: bfloat16 [320, 320, 128], P('row', 'col'), may hold values from -24 to 24
- genuine_homolog_total: int32 [1], replicated, may hold values from 1 to 64
- genuine_chain_length: int32 [1], replicated, may hold values from 160 to 320
- tensor_product_matrices: bfloat16 [1, 64, 64], replicated, may hold values from -0.75 to 0.75
- tensor_product_final: bfloat16 [1, 1024, 128], replicated, may hold values from -0.75 to 0.75
- mixing_value_gate_matrix: bfloat16 [1, 64, 512], replicated, may hold values from -0.75 to 0.75
- mixing_logit_matrix: bfloat16 [1, 128, 8], replicated
- mixing_final_matrix: bfloat16 [1, 256, 64], replicated, may hold values from -1.5 to 1.5
- feedforward_gate_expand: bfloat16 [1, 128, 1024], replicated, may hold values from -0.5 to 0.5
- feedforward_shrink_matrix: bfloat16 [1, 512, 128], replicated, may hold values from -0.25 to 0.25
Outputs:
- msa_out: bfloat16 [64, 320, 64], P('row', 'col')
- pair_out: bfloat16 [320, 320, 128], P('row', 'col')
The draws below stay inside these ranges and needn't reach their ends.
Inputs may be any that keep to these rules, and one draw needn't show every extreme that they name: Sequences from genuine_homolog_total on are padding. Residues from genuine_chain_length on are padding.
All inputs are finite; a program needn't handle non-finite values.
Results may differ from the reference program's by a relative error of at most 0.0065.
The reference program's roundings to bfloat16 on the way count: a program that leaves them out, or rounds other values in their place, can miss the bound.
Values may be sent and summed in bfloat16 or wider, within the bound.
A program may use at most 64 MiB of HBM per device.

```python
import math
import jax
import jax.numpy as jnp
from jax import lax

ALIGNED_FEATURES = 64
C_Z = 128
PRODUCT_FEATURES = 32
ATTENTION_GROUPS = 8
GROUP_FEATURES = 32
TRANS = 512
MODULE_REPEATS = 1
HOMOLOG_TOTAL = 64
CHAIN_LENGTH = 320


def pair_law(key):
    base = jax.random.fold_in(key, 7011)
    key_dirs = jax.random.fold_in(base, 0)
    key_field = jax.random.fold_in(base, 1)
    key_rows = jax.random.fold_in(base, 3)
    key_noise = jax.random.fold_in(base, 4)
    key_rest = jax.random.fold_in(base, 6)
    raw = jax.random.normal(key_dirs, (MODULE_REPEATS, C_Z, ATTENTION_GROUPS), jnp.float32)
    raw = raw - jnp.mean(raw, axis=1, keepdims=True)
    basis = jnp.linalg.qr(raw.transpose(1, 0, 2).reshape(C_Z, MODULE_REPEATS * ATTENTION_GROUPS))[0]
    directions = basis.reshape(C_Z, MODULE_REPEATS, ATTENTION_GROUPS).transpose(1, 0, 2) * math.sqrt(C_Z)
    rest = jax.random.normal(key_rest, (MODULE_REPEATS, C_Z, ATTENTION_GROUPS), jnp.float32) * (2.0 / math.sqrt(C_Z))
    field = jnp.clip(jax.random.normal(key_field, (CHAIN_LENGTH, CHAIN_LENGTH, C_Z), jnp.float32), -6.0, 6.0)
    strength = 110.0 * jnp.ones((MODULE_REPEATS, 1, ATTENTION_GROUPS), jnp.float32)
    weights = directions * (strength / C_Z) + rest
    coords = jnp.einsum('ijc,ck->ijk', field, basis)
    field = field - 0.9 * jnp.einsum('ijk,ck->ijc', coords, basis)
    field = jnp.clip(field, -24.0, 24.0)
    picks = jax.random.permutation(key_rows, CHAIN_LENGTH)
    for block_id in range(MODULE_REPEATS):
        for head_id in range(ATTENTION_GROUPS):
            slot = block_id * ATTENTION_GROUPS + head_id
            direction = directions[block_id, :, head_id]
            noise = jax.random.normal(jax.random.fold_in(key_noise, slot), (2, CHAIN_LENGTH, C_Z), jnp.float32)
            high_row = picks[2 * slot]
            low_row = picks[2 * slot + 1]
            field = field.at[high_row].set(jnp.clip(6.0 * direction[None, :] + 0.3 * noise[0], -24.0, 24.0))
            field = field.at[low_row].set(jnp.clip(-6.0 * direction[None, :] + 0.3 * noise[1], -24.0, 24.0))
    return (weights, field)


def draw_contact_matrix(key, part):
    return pair_law(key)[1].astype(jnp.bfloat16)


def draw_mixing_logit_matrix(key, part):
    return pair_law(key)[0].astype(jnp.bfloat16)


def level_of(key, dims, cuts, low, largest):
    factor_of = 1.0
    for position, parts in cuts:
        draws = jax.random.uniform(jax.random.fold_in(jax.random.fold_in(key, 6), position), (parts,), jnp.float32, low / len(cuts), largest / len(cuts))
        factor_of = factor_of * jnp.repeat(jnp.exp(draws), dims[position] // parts).reshape((-1,) + (1,) * (len(dims) - 1 - position))
    return factor_of


def gaussian(rng, dims, scale, limit, cuts=(), kind=jnp.bfloat16):
    entries = scale * jax.random.normal(rng, dims, jnp.float32)
    if cuts:
        entries = entries * level_of(rng, dims, cuts, -0.22, 0.18)
    return jnp.clip(entries, -limit, limit).astype(kind)


def setup_inputs(seed: int = 0) -> dict:
    arg_keys = jax.random.split(jax.random.key(seed), 12)
    return {
        "homolog_matrix": gaussian(arg_keys[0], (HOMOLOG_TOTAL, CHAIN_LENGTH, ALIGNED_FEATURES), 1.0, 6.0, ((0, 8), (1, 4))),
        "contact_matrix": draw_contact_matrix(jax.random.fold_in(arg_keys[11], 71), 0),
        "genuine_homolog_total": jax.random.randint(arg_keys[2], (1,), 1, HOMOLOG_TOTAL + 1).astype(jnp.int32),
        "genuine_chain_length": jax.random.randint(arg_keys[3], (1,), CHAIN_LENGTH // 2, CHAIN_LENGTH + 1).astype(jnp.int32),
        "tensor_product_matrices": gaussian(arg_keys[4], (MODULE_REPEATS, ALIGNED_FEATURES, 2 * PRODUCT_FEATURES), ALIGNED_FEATURES ** -0.5, 0.75),
        "tensor_product_final": gaussian(arg_keys[5], (MODULE_REPEATS, PRODUCT_FEATURES * PRODUCT_FEATURES, C_Z), (PRODUCT_FEATURES * PRODUCT_FEATURES // 16) ** -0.5, 0.75),
        "mixing_value_gate_matrix": gaussian(arg_keys[6], (MODULE_REPEATS, ALIGNED_FEATURES, 2 * ATTENTION_GROUPS * GROUP_FEATURES), ALIGNED_FEATURES ** -0.5, 0.75),
        "mixing_logit_matrix": draw_mixing_logit_matrix(jax.random.fold_in(arg_keys[11], 71), 0),
        "mixing_final_matrix": gaussian(arg_keys[8], (MODULE_REPEATS, ATTENTION_GROUPS * GROUP_FEATURES, ALIGNED_FEATURES), (ATTENTION_GROUPS * GROUP_FEATURES // 16) ** -0.5, 1.5),
        "feedforward_gate_expand": gaussian(arg_keys[9], (MODULE_REPEATS, C_Z, 2 * TRANS), C_Z ** -0.5, 0.5),
        "feedforward_shrink_matrix": gaussian(arg_keys[10], (MODULE_REPEATS, TRANS, C_Z), TRANS ** -0.5, 0.25),
    }


EPSILON = 1e-05
MASKED = -1000000000.0

def standardize_features(field):
    field = field.astype(jnp.float32)
    center = field - lax.optimization_barrier(jnp.mean(field, axis=-1, keepdims=True))
    spread = lax.optimization_barrier(jnp.mean(center * center, axis=-1, keepdims=True))
    return center * lax.rsqrt(spread + EPSILON)

def reference(homolog_matrix, contact_matrix, genuine_homolog_total, genuine_chain_length, tensor_product_matrices, tensor_product_final, mixing_value_gate_matrix, mixing_logit_matrix, mixing_final_matrix, feedforward_gate_expand, feedforward_shrink_matrix):
    hidden_width = ATTENTION_GROUPS * GROUP_FEATURES
    row_blocks = CHAIN_LENGTH // 8
    seq_float = (jnp.arange(HOMOLOG_TOTAL, dtype=jnp.int32) < genuine_homolog_total[0]).astype(jnp.float32)
    res_valid = jnp.arange(CHAIN_LENGTH, dtype=jnp.int32) < genuine_chain_length[0]
    res_float = res_valid.astype(jnp.float32)
    divisor = jnp.maximum(genuine_homolog_total[0].astype(jnp.float32) * res_float[:, None] * res_float[None, :], 1.0)
    starts = jnp.arange(row_blocks, dtype=jnp.int32) * 8
    for block_id in range(MODULE_REPEATS):
        standardized_source = standardize_features(homolog_matrix).astype(jnp.bfloat16)
        reshaped_tensor = standardized_source.reshape(HOMOLOG_TOTAL * CHAIN_LENGTH, ALIGNED_FEATURES)
        projected = jnp.dot(reshaped_tensor.astype(jnp.float32), tensor_product_matrices[block_id].astype(jnp.float32), preferred_element_type=jnp.float32).reshape(HOMOLOG_TOTAL, CHAIN_LENGTH, 2 * PRODUCT_FEATURES)
        projected = (projected * (seq_float[:, None, None] * res_float[None, :, None])).astype(jnp.bfloat16)
        left = projected[:, :, :PRODUCT_FEATURES]
        right = projected[:, :, PRODUCT_FEATURES:].reshape(HOMOLOG_TOTAL, CHAIN_LENGTH * PRODUCT_FEATURES)
        outer_weight = tensor_product_final[block_id]

        def outer_rows(inputs):
            start, pair_rows = inputs
            rows = lax.dynamic_slice_in_dim(left, start, 8, 1).reshape(HOMOLOG_TOTAL, 8 * PRODUCT_FEATURES)
            product = lax.dot_general(rows.astype(jnp.float32), right.astype(jnp.float32), (((0,), (0,)), ((), ())), preferred_element_type=jnp.float32)
            product = product.reshape(8, PRODUCT_FEATURES, CHAIN_LENGTH, PRODUCT_FEATURES).transpose(0, 2, 1, 3).reshape(8, CHAIN_LENGTH, PRODUCT_FEATURES * PRODUCT_FEATURES)
            scale = lax.dynamic_slice_in_dim(divisor, start, 8, 0)
            outer = (product / scale[:, :, None]).astype(jnp.bfloat16)
            update = jnp.dot(outer.reshape(8 * CHAIN_LENGTH, PRODUCT_FEATURES * PRODUCT_FEATURES).astype(jnp.float32), outer_weight.astype(jnp.float32), preferred_element_type=jnp.float32)
            return (pair_rows.astype(jnp.float32) + update.reshape(8, CHAIN_LENGTH, C_Z)).astype(jnp.bfloat16)
        contact_matrix = lax.map(outer_rows, (starts, contact_matrix.reshape(row_blocks, 8, CHAIN_LENGTH, C_Z))).reshape(CHAIN_LENGTH, CHAIN_LENGTH, C_Z)
        bias_weight = mixing_logit_matrix[block_id]

        def norm_rows(pair_rows):
            normed_rows = standardize_features(pair_rows).astype(jnp.bfloat16)
            logit_rows = jnp.dot(normed_rows.reshape(8 * CHAIN_LENGTH, C_Z).astype(jnp.float32), bias_weight.astype(jnp.float32), preferred_element_type=jnp.float32)
            return (normed_rows, logit_rows.reshape(8, CHAIN_LENGTH, ATTENTION_GROUPS))
        pair_normed, logits = lax.map(norm_rows, contact_matrix.reshape(row_blocks, 8, CHAIN_LENGTH, C_Z))
        logits = jnp.where(res_valid[None, :, None], logits.reshape(CHAIN_LENGTH, CHAIN_LENGTH, ATTENTION_GROUPS), MASKED)
        peak = lax.optimization_barrier(jnp.max(logits, axis=1, keepdims=True))
        expo = jnp.exp(logits - peak)
        weights = (expo / lax.optimization_barrier(jnp.sum(expo, axis=1, keepdims=True))).astype(jnp.bfloat16)
        both = jnp.dot(reshaped_tensor.astype(jnp.float32), mixing_value_gate_matrix[block_id].astype(jnp.float32), preferred_element_type=jnp.float32).reshape(HOMOLOG_TOTAL, CHAIN_LENGTH, 2 * hidden_width)
        values = both[:, :, :hidden_width].astype(jnp.bfloat16).reshape(HOMOLOG_TOTAL, CHAIN_LENGTH, ATTENTION_GROUPS, GROUP_FEATURES)
        gate = jax.nn.sigmoid(both[:, :, hidden_width:])
        averaged = jnp.einsum('ijh,sjhc->sihc', weights.astype(jnp.float32), values.astype(jnp.float32))
        gated = (gate * averaged.reshape(HOMOLOG_TOTAL, CHAIN_LENGTH, hidden_width)).astype(jnp.bfloat16)
        contact_increment = jnp.dot(gated.reshape(HOMOLOG_TOTAL * CHAIN_LENGTH, hidden_width).astype(jnp.float32), mixing_final_matrix[block_id].astype(jnp.float32), preferred_element_type=jnp.float32)
        homolog_matrix = (homolog_matrix.astype(jnp.float32) + contact_increment.reshape(HOMOLOG_TOTAL, CHAIN_LENGTH, ALIGNED_FEATURES)).astype(jnp.bfloat16)
        up_weight = feedforward_gate_expand[block_id]
        down_weight = feedforward_shrink_matrix[block_id]

        def transition_rows(inputs):
            pair_rows, normed_rows = inputs
            hidden = jnp.dot(normed_rows.reshape(8 * CHAIN_LENGTH, C_Z).astype(jnp.float32), up_weight.astype(jnp.float32), preferred_element_type=jnp.float32)
            active = (jax.nn.silu(hidden[:, :TRANS]) * hidden[:, TRANS:]).astype(jnp.bfloat16)
            update = jnp.dot(active.astype(jnp.float32), down_weight.astype(jnp.float32), preferred_element_type=jnp.float32)
            return (pair_rows.astype(jnp.float32) + update.reshape(8, CHAIN_LENGTH, C_Z)).astype(jnp.bfloat16)
        contact_matrix = lax.map(transition_rows, (contact_matrix.reshape(row_blocks, 8, CHAIN_LENGTH, C_Z), pair_normed)).reshape(CHAIN_LENGTH, CHAIN_LENGTH, C_Z)
    return (homolog_matrix, contact_matrix)
```

```python
import functools

import jax
import jax.numpy as jnp
from jax import lax
from jax.experimental import pallas as pl
from jax.experimental.pallas import tpu as pltpu
from jax.sharding import PartitionSpec as P

EPSILON = 1e-05
MASKED = -1000000000.0
MESH = pl.DeviceIdType.MESH
LANES = 128
BF16 = jnp.bfloat16
F32 = jnp.float32


def standardize_features(field):
    field = field.astype(F32)
    center = field - jnp.mean(field, axis=-1, keepdims=True)
    spread = jnp.mean(center * center, axis=-1, keepdims=True)
    return center * lax.rsqrt(spread + EPSILON)


def kernel(
    dims,
    seqs_ref, length_ref,
    right_ref, left_ref, normed_ref, homolog_ref, pair_ref,
    outer_w_ref, value_w_ref, gate_w_ref, logit_w_ref, final_w_ref, up_ref, down_ref,
    msa_ref, out_ref,
    right_buf, left_buf, normed_buf, logit_send, logit_buf,
    right_all, left_all, product, pair_new, pair_normed, values, gates, gated,
    s_right, r_right, s_left, r_left, s_norm, r_norm, s_logit, r_logit,
):
    R, C, ratio, rows, cols, width, heads, chunks = dims
    r = lax.axis_index("row")
    c = lax.axis_index("col")
    home = r // ratio

    barrier = pltpu.get_barrier_semaphore()

    def greet(row, col):
        pl.semaphore_signal(barrier, inc=1, device_id=(row, col), device_id_type=MESH)

    for t in range(1, R):
        greet((r + t) % R, c)
    for t in range(1, C):
        greet(r, (c + t) % C)
    for t in range(R):
        row = (r + t) % R

        @pl.when(jnp.logical_not((row == r) & (home == c)))
        def _():
            greet(row, home)

    for h in range(ratio):
        for t in range(C):
            row, col = c * ratio + h, (c + t) % C

            @pl.when(jnp.logical_not((row == r) & (col == c)))
            def _():
                greet(row, col)

    own = jnp.where(home == c, 1, 0)
    pl.semaphore_wait(barrier, (R - 1) + (C - 1) + 2 * R - 2 * own)

    def right_copy(t):
        return pltpu.make_async_remote_copy(
            src_ref=right_ref, dst_ref=right_buf.at[r],
            send_sem=s_right.at[t], recv_sem=r_right.at[r],
            device_id=((r + t) % R, c), device_id_type=MESH)

    def left_copy(h, t):
        return pltpu.make_async_remote_copy(
            src_ref=left_ref.at[h], dst_ref=left_buf.at[r],
            send_sem=s_left.at[h, t], recv_sem=r_left.at[r],
            device_id=(c * ratio + h, (c + t) % C), device_id_type=MESH)

    def norm_copy(t):
        return pltpu.make_async_remote_copy(
            src_ref=normed_ref, dst_ref=normed_buf.at[c],
            send_sem=s_norm.at[t], recv_sem=r_norm.at[c],
            device_id=(r, (c + t) % C), device_id_type=MESH)

    def logit_copy(k, t):
        return pltpu.make_async_remote_copy(
            src_ref=logit_send.at[k], dst_ref=logit_buf.at[r % ratio, c, k],
            send_sem=s_logit.at[k, t], recv_sem=r_logit.at[r % ratio, c, k],
            device_id=((r + t) % R, home), device_id_type=MESH)

    for h in range(ratio):
        for t in range(C):
            mine = (c * ratio + h == r) & (t == 0)

            @pl.when(jnp.logical_not(mine))
            def _():
                left_copy(h, t).start()

            @pl.when(mine)
            def _():
                left_buf[r] = left_ref[h]

    for t in range(1, R):
        right_copy(t).start()
    for t in range(1, C):
        norm_copy(t).start()
    right_buf[r] = right_ref[...]
    normed_buf[c] = normed_ref[...]

    def wait_left(src):
        pltpu.make_async_remote_copy(
            src_ref=left_ref.at[0], dst_ref=left_buf.at[src],
            send_sem=s_left.at[0, 0], recv_sem=r_left.at[src],
            device_id=(src, home), device_id_type=MESH).wait_recv()

    def wait_right(src):
        pltpu.make_async_remote_copy(
            src_ref=right_ref, dst_ref=right_buf.at[src],
            send_sem=s_right.at[0], recv_sem=r_right.at[src],
            device_id=(src, c), device_id_type=MESH).wait_recv()

    def wait_norm(src):
        pltpu.make_async_remote_copy(
            src_ref=normed_ref, dst_ref=normed_buf.at[src],
            send_sem=s_norm.at[0], recv_sem=r_norm.at[src],
            device_id=(r, src), device_id_type=MESH).wait_recv()

    groups = gates.shape[1] // (heads * LANES)
    group_width = width // groups
    for g in range(groups):
        part = jnp.dot(
            normed_ref[:, g * group_width:(g + 1) * group_width], gate_w_ref[...],
            preferred_element_type=F32)
        for h in range(heads):
            at = (h * groups + g) * LANES
            gates[:, at:at + LANES] = jax.nn.sigmoid(part[:, h * LANES:(h + 1) * LANES])
    values[...] = jnp.zeros_like(values)
    logit_send[...] = jnp.zeros_like(logit_send)

    for src in range(R):
        @pl.when(jnp.logical_not((src == r) & (home == c)))
        def _():
            wait_left(src)

    left_t = left_buf[...].astype(F32).reshape(R * left_buf.shape[1], left_buf.shape[2]).T
    left_all[...] = left_t.astype(BF16)
    for t in range(1, R):
        wait_right((r + t) % R)
    right_all[...] = right_buf[...].astype(F32).reshape(right_all.shape).astype(BF16)

    inverse = 1.0 / jnp.maximum(seqs_ref[0].astype(F32), 1.0)
    ch = product.shape[1] // (right_all.shape[1] // LANES)

    def send_logits(k):
        for t in range(R):
            if t > 0:
                logit_copy(k, t).start()
            else:
                @pl.when(home == c)
                def _():
                    logit_buf[r % ratio, c, k] = logit_send[k]

                @pl.when(home != c)
                def _():
                    logit_copy(k, 0).start()

    def outer_step(k, carry):
        @pl.when(k > 0)
        def _():
            send_logits(k - 1)

        lhs = left_all[pl.ds(pl.multiple_of(k * 8 * ch, 8 * ch), 8 * ch), :]
        for d in range(0, right_all.shape[1] // LANES, 2):
            p = jnp.dot(lhs, right_all[:, d * LANES:(d + 2) * LANES], preferred_element_type=F32)
            p = (p * inverse).astype(BF16)
            for e in range(2):
                product[:, (d + e) * ch:(d + e + 1) * ch, :] = p[
                    :, e * LANES:(e + 1) * LANES].reshape(8, ch, LANES)
        for q in range(0, 8, 2):
            both = jnp.concatenate([product[q], product[q + 1]], axis=1)
            update = jnp.dot(outer_w_ref[...], both, preferred_element_type=F32)
            for e in range(2):
                i = k * 8 + q + e
                step = update[:, e * LANES:(e + 1) * LANES].T[:cols]
                pair = (pair_ref[i].astype(F32) + step).astype(BF16)
                pair_new[i] = pair
                normed = standardize_features(pair).astype(BF16)
                pair_normed[i] = normed
                logits = lax.dot_general(
                    logit_w_ref[...], normed, (((1,), (1,)), ((), ())),
                    preferred_element_type=F32)
                logit_send[k, :, q + e, 0:cols] = logits
        return carry

    lax.fori_loop(0, chunks, outer_step, 0)
    send_logits(chunks - 1)

    trans = down_ref.shape[0]

    def transition_step(k, carry):
        normed = pair_normed[pl.ds(k * 4, 4)].reshape(4 * cols, LANES)
        hidden = jnp.dot(normed, up_ref[...], preferred_element_type=F32)
        front, back = hidden[:, :trans], hidden[:, trans:]
        active = (front / (1.0 + jnp.exp(-front)) * back).astype(BF16)
        update = jnp.dot(active, down_ref[...], preferred_element_type=F32)
        pair = pair_new[pl.ds(k * 4, 4)].astype(F32) + update.reshape(4, cols, LANES)
        out_ref[pl.ds(k * 4, 4)] = pair.astype(BF16)
        return carry

    lax.fori_loop(0, rows // 4, transition_step, 0)

    for t in range(1, C):
        wait_norm((c + t) % C)
    for src in range(C):
        for g in range(groups):
            part = jnp.dot(
                normed_buf[src, :, g * group_width:(g + 1) * group_width], value_w_ref[...],
                preferred_element_type=F32).astype(BF16)
            for h in range(heads):
                at = (h * groups + g) * LANES
                values[src * LANES:src * LANES + cols, at:at + LANES] = part[
                    :, h * LANES:(h + 1) * LANES]

    for h in range(ratio):
        for src in range(C):
            @pl.when(jnp.logical_not((c * ratio + h == r) & (src == c)))
            def _():
                for k in range(chunks):
                    pltpu.make_async_remote_copy(
                        src_ref=logit_send.at[k], dst_ref=logit_buf.at[h, src, k],
                        send_sem=s_logit.at[k, 0], recv_sem=r_logit.at[h, src, k],
                        device_id=(r, home), device_id_type=MESH).wait_recv()

    lane = lax.broadcasted_iota(jnp.int32, (cols, C * LANES), 1)
    valid = (lane % LANES < cols) & (lane // LANES * cols + lane % LANES < length_ref[0])
    span = groups * LANES
    for h in range(heads):
        logits = jnp.concatenate([
            jnp.concatenate(
                [logit_buf[half, src, :, h].reshape(rows, LANES) for src in range(C)], axis=1)
            for half in range(ratio)], axis=0)
        logits = jnp.where(valid, logits, MASKED)
        expo = jnp.exp(logits - jnp.max(logits, axis=1, keepdims=True))
        weights = (expo / jnp.sum(expo, axis=1, keepdims=True)).astype(BF16)
        mean = jnp.dot(weights, values[:, h * span:(h + 1) * span], preferred_element_type=F32)
        mixed = (gates[:, h * span:(h + 1) * span] * mean).astype(BF16)
        for g in range(groups):
            at = (g * heads + h) * LANES
            gated[:, at:at + LANES] = mixed[:, g * LANES:(g + 1) * LANES]
    for g in range(groups):
        part = jnp.dot(
            gated[:, g * heads * LANES:(g + 1) * heads * LANES], final_w_ref[...],
            preferred_element_type=F32)
        sl = slice(g * group_width, (g + 1) * group_width)
        msa_ref[:, sl] = (homolog_ref[:, sl].astype(F32) + part).astype(BF16)

    for t in range(1, R):
        right_copy(t).wait_send()
    for t in range(1, C):
        norm_copy(t).wait_send()
    for h in range(ratio):
        for t in range(C):
            @pl.when(jnp.logical_not((c * ratio + h == r) & (t == 0)))
            def _():
                left_copy(h, t).wait_send()

    def finish(k, carry):
        for t in range(1, R):
            logit_copy(k, t).wait_send()

        @pl.when(home != c)
        def _():
            logit_copy(k, 0).wait_send()

        return carry

    lax.fori_loop(0, chunks, finish, 0)


def local(
    R,
    C,
    homolog_matrix,
    contact_matrix,
    genuine_homolog_total,
    genuine_chain_length,
    tensor_product_matrices,
    tensor_product_final,
    mixing_value_gate_matrix,
    mixing_logit_matrix,
    mixing_final_matrix,
    feedforward_gate_expand,
    feedforward_shrink_matrix,
):
    seqs, cols, feats = homolog_matrix.shape
    rows, _, pair_width = contact_matrix.shape
    ch = tensor_product_matrices.shape[2] // 2
    heads = mixing_logit_matrix.shape[2]
    hidden = mixing_final_matrix.shape[1]
    head_width = hidden // heads
    ratio = R // C
    chunks = rows // 8
    pack = LANES // head_width
    groups = seqs // pack
    r = lax.axis_index("row")
    c = lax.axis_index("col")
    seq_ids = r * seqs + jnp.arange(seqs, dtype=jnp.int32)
    res_ids = c * cols + jnp.arange(cols, dtype=jnp.int32)
    seq_float = (seq_ids < genuine_homolog_total[0]).astype(F32)
    res_float = (res_ids < genuine_chain_length[0]).astype(F32)
    flipped = homolog_matrix.transpose(1, 0, 2)
    normed = standardize_features(homolog_matrix).astype(BF16)
    normed_flat = normed.transpose(1, 0, 2).reshape(cols, seqs * feats)
    left_w = tensor_product_matrices[0][:, :ch]
    right_w = tensor_product_matrices[0][:, ch:]
    right = jnp.einsum("sjf,fd->sdj", normed, right_w, preferred_element_type=F32)
    right = (right * (seq_float[:, None, None] * res_float[None, None, :])).astype(BF16)
    right = jnp.pad(right, ((0, 0), (0, 0), (0, LANES - cols))).reshape(seqs, ch * LANES)
    left = jnp.einsum("sjf,fc->sjc", normed, left_w, preferred_element_type=F32)
    left = (left * (seq_float[:, None, None] * res_float[None, :, None])).astype(BF16)
    left = left.reshape(seqs, ratio, rows * ch).transpose(1, 0, 2)
    outer_w = tensor_product_final[0].reshape(ch, ch, pair_width).transpose(2, 1, 0)
    outer_w = outer_w.reshape(pair_width, ch * ch)
    same = jnp.eye(pack, dtype=BF16)
    vg = mixing_value_gate_matrix[0].reshape(feats, 2, heads, head_width)
    spread = vg[None, :, :, :, None, :] * same[:, None, None, None, :, None]
    spread = spread.reshape(pack * feats, 2, heads * LANES)
    final = mixing_final_matrix[0].reshape(heads, 1, head_width, 1, feats)
    final = (final * same[None, :, None, :, None]).reshape(heads * LANES, pack * feats)
    dims = (R, C, ratio, rows, cols, seqs * feats, heads, chunks)
    vmem = pl.BlockSpec(memory_space=pltpu.VMEM)
    smem = pl.BlockSpec(memory_space=pltpu.SMEM)
    dma = pltpu.SemaphoreType.DMA
    msa, pair_out = pl.pallas_call(
        functools.partial(kernel, dims),
        out_shape=(
            jax.ShapeDtypeStruct((cols, seqs * feats), BF16),
            jax.ShapeDtypeStruct(contact_matrix.shape, BF16),
        ),
        in_specs=[smem] * 2 + [vmem] * 12,
        out_specs=(vmem, vmem),
        scratch_shapes=[
            pltpu.VMEM((R, seqs, ch * LANES), BF16),
            pltpu.VMEM((R, seqs, rows * ch), BF16),
            pltpu.VMEM((C, cols, seqs * feats), BF16),
            pltpu.VMEM((chunks, heads, 8, LANES), F32),
            pltpu.VMEM((ratio, C, chunks, heads, 8, LANES), F32),
            pltpu.VMEM((R * seqs, ch * LANES), BF16),
            pltpu.VMEM((rows * ch, R * seqs), BF16),
            pltpu.VMEM((8, ch * ch, LANES), BF16),
            pltpu.VMEM((rows, cols, pair_width), BF16),
            pltpu.VMEM((rows, cols, pair_width), BF16),
            pltpu.VMEM((C * LANES, heads * groups * LANES), BF16),
            pltpu.VMEM((cols, heads * groups * LANES), F32),
            pltpu.VMEM((cols, heads * groups * LANES), BF16),
            dma((R,)), dma((R,)), dma((ratio, C)), dma((R,)), dma((C,)), dma((C,)),
            dma((chunks, R)), dma((ratio, C, chunks)),
        ],
        compiler_params=pltpu.CompilerParams(
            collective_id=0, has_side_effects=True, vmem_limit_bytes=60 * 1024 * 1024
        ),
        name="msa_block",
    )(
        genuine_homolog_total, genuine_chain_length,
        right, left, normed_flat, flipped.reshape(cols, seqs * feats), contact_matrix,
        outer_w, spread[:, 0], spread[:, 1], mixing_logit_matrix[0].T, final,
        feedforward_gate_expand[0], feedforward_shrink_matrix[0],
    )
    return (msa.reshape(cols, seqs, feats).transpose(1, 0, 2), pair_out)


def solution(mesh):
    in_specs = (P("row", "col", None), P("row", "col", None)) + (P(),) * 9
    out_specs = (P("row", "col", None), P("row", "col", None))
    body = functools.partial(local, mesh.shape["row"], mesh.shape["col"])
    return jax.shard_map(body, mesh=mesh, in_specs=in_specs, out_specs=out_specs, check_vma=False)
```

```python
import functools

import jax
import jax.numpy as jnp
from jax import lax
from jax.experimental import pallas as pl
from jax.experimental.pallas import tpu as pltpu
from jax.sharding import PartitionSpec as P

EPSILON = 1e-05
MASKED = -1000000000.0
MESH = pl.DeviceIdType.MESH
LANES = 128
BF16 = jnp.bfloat16
F32 = jnp.float32


def standardize_features(field):
    field = field.astype(F32)
    center = field - jnp.mean(field, axis=-1, keepdims=True)
    spread = jnp.mean(center * center, axis=-1, keepdims=True)
    return center * lax.rsqrt(spread + EPSILON)


def flip(index, mask):
    bit = 1
    while bit <= mask:
        if mask & bit:
            index = index + bit - 2 * bit * ((index // bit) % 2)
        bit *= 2
    return index


def kernel(
    dims,
    seqs_ref, length_ref,
    right_ref, left_ref, normed_ref, homolog_ref, pair_ref,
    outer_w_ref, value_w_ref, gate_w_ref, logit_w_ref, final_w_ref, up_ref, down_ref,
    msa_ref, out_ref,
    right_buf, left_buf, normed_buf, logit_send, logit_buf, weight_buf,
    right_all, left_all, product, pair_new, pair_normed, values, gates, gated,
    s_right, r_right, s_left, r_left, s_norm, r_norm, s_logit, r_logit, s_weight, r_weight,
):
    R, C, ratio, rows, cols, width, heads, chunks = dims
    r = lax.axis_index("row")
    c = lax.axis_index("col")
    home = r // ratio

    barrier = pltpu.get_barrier_semaphore()

    def greet(row, col):
        pl.semaphore_signal(barrier, inc=1, device_id=(row, col), device_id_type=MESH)

    for t in range(1, R):
        greet((r + t) % R, c)
    for t in range(1, C):
        greet(r, (c + t) % C)
    for t in range(R):
        row = (r + t) % R

        @pl.when(jnp.logical_not((row == r) & (home == c)))
        def _():
            greet(row, home)

    for h in range(ratio):
        for t in range(C):
            row, col = c * ratio + h, (c + t) % C

            @pl.when(jnp.logical_not((row == r) & (col == c)))
            def _():
                greet(row, col)

    own = jnp.where(home == c, 1, 0)
    pl.semaphore_wait(barrier, (R - 1) + (C - 1) + 2 * R - 2 * own)

    def right_copy(n):
        root = flip(r, n & (n - 1))
        return pltpu.make_async_remote_copy(
            src_ref=right_buf.at[root] if n & (n - 1) else right_ref,
            dst_ref=right_buf.at[root],
            send_sem=s_right.at[n], recv_sem=r_right.at[n],
            device_id=(flip(r, n & -n), c), device_id_type=MESH)

    def left_copy(h, t):
        return pltpu.make_async_remote_copy(
            src_ref=left_ref.at[h], dst_ref=left_buf.at[r],
            send_sem=s_left.at[h, t], recv_sem=r_left.at[r],
            device_id=(c * ratio + h, (c + t) % C), device_id_type=MESH)

    def norm_copy(t):
        return pltpu.make_async_remote_copy(
            src_ref=normed_ref, dst_ref=normed_buf.at[c],
            send_sem=s_norm.at[t], recv_sem=r_norm.at[c],
            device_id=(r, (c + t) % C), device_id_type=MESH)

    def logit_copy(k):
        return pltpu.make_async_remote_copy(
            src_ref=logit_send.at[k], dst_ref=logit_buf.at[c, k],
            send_sem=s_logit.at[k], recv_sem=r_logit.at[c, k],
            device_id=(r, home), device_id_type=MESH)

    steps = [R >> (e + 1) for e in range(R.bit_length() - 1)]

    def weight_copy(half, p, e):
        return pltpu.make_async_remote_copy(
            src_ref=weight_buf.at[half, p], dst_ref=weight_buf.at[half, p],
            send_sem=s_weight.at[half, p, e], recv_sem=r_weight.at[half, p],
            device_id=(flip(r, steps[e]), c), device_id_type=MESH)

    def relation(half):
        root = c * ratio + half
        total = 0
        for bit in steps:
            total = total + bit * (((r // bit) % 2 + (root // bit) % 2) % 2)
        return total

    for h in range(ratio):
        for t in range(C):
            mine = (c * ratio + h == r) & (t == 0)

            @pl.when(jnp.logical_not(mine))
            def _():
                left_copy(h, t).start()

            @pl.when(mine)
            def _():
                left_buf[r] = left_ref[h]

    for bit in steps:
        right_copy(bit).start()
    for t in range(1, C):
        norm_copy(t).start()
    right_buf[r] = right_ref[...]
    normed_buf[c] = normed_ref[...]

    def wait_left(src):
        pltpu.make_async_remote_copy(
            src_ref=left_ref.at[0], dst_ref=left_buf.at[src],
            send_sem=s_left.at[0, 0], recv_sem=r_left.at[src],
            device_id=(src, home), device_id_type=MESH).wait_recv()

    def wait_right(n):
        pltpu.make_async_remote_copy(
            src_ref=right_ref, dst_ref=right_buf.at[flip(r, n)],
            send_sem=s_right.at[n], recv_sem=r_right.at[n],
            device_id=(flip(r, n & -n), c), device_id_type=MESH).wait_recv()

    def wait_norm(src):
        pltpu.make_async_remote_copy(
            src_ref=normed_ref, dst_ref=normed_buf.at[src],
            send_sem=s_norm.at[0], recv_sem=r_norm.at[src],
            device_id=(r, src), device_id_type=MESH).wait_recv()

    for n in sorted(range(1, R), key=lambda n: (bin(n).count("1"), -(n & -n))):
        wait_right(n)
        for bit in steps:
            if bit < n & -n:
                right_copy(n + bit).start()

    groups = gates.shape[1] // (heads * LANES)
    group_width = width // groups
    for g in range(groups):
        part = jnp.dot(
            normed_ref[:, g * group_width:(g + 1) * group_width], gate_w_ref[...],
            preferred_element_type=F32)
        for h in range(heads):
            at = (h * groups + g) * LANES
            gates[:, at:at + LANES] = jax.nn.sigmoid(part[:, h * LANES:(h + 1) * LANES])
    values[...] = jnp.zeros_like(values)
    logit_send[...] = jnp.zeros_like(logit_send)

    for src in range(R):
        @pl.when(jnp.logical_not((src == r) & (home == c)))
        def _():
            wait_left(src)

    left_t = left_buf[...].astype(F32).reshape(R * left_buf.shape[1], left_buf.shape[2]).T
    left_all[...] = left_t.astype(BF16)
    right_all[...] = right_buf[...].astype(F32).reshape(right_all.shape).astype(BF16)

    inverse = 1.0 / jnp.maximum(seqs_ref[0].astype(F32), 1.0)
    ch = product.shape[1] // (right_all.shape[1] // LANES)

    def send_logits(k):
        @pl.when(home == c)
        def _():
            logit_buf[c, k] = logit_send[k]

        @pl.when(home != c)
        def _():
            logit_copy(k).start()

    def outer_step(k, carry):
        @pl.when(k > 0)
        def _():
            send_logits(k - 1)

        lhs = left_all[pl.ds(pl.multiple_of(k * 8 * ch, 8 * ch), 8 * ch), :]
        for d in range(0, right_all.shape[1] // LANES, 2):
            p = jnp.dot(lhs, right_all[:, d * LANES:(d + 2) * LANES], preferred_element_type=F32)
            p = (p * inverse).astype(BF16)
            for e in range(2):
                product[:, (d + e) * ch:(d + e + 1) * ch, :] = p[
                    :, e * LANES:(e + 1) * LANES].reshape(8, ch, LANES)
        for q in range(0, 8, 2):
            both = jnp.concatenate([product[q], product[q + 1]], axis=1)
            update = jnp.dot(outer_w_ref[...], both, preferred_element_type=F32)
            for e in range(2):
                i = k * 8 + q + e
                step = update[:, e * LANES:(e + 1) * LANES].T[:cols]
                pair = (pair_ref[i].astype(F32) + step).astype(BF16)
                pair_new[i] = pair
                normed = standardize_features(pair).astype(BF16)
                pair_normed[i] = normed
                logits = lax.dot_general(
                    logit_w_ref[...], normed, (((1,), (1,)), ((), ())),
                    preferred_element_type=F32)
                logit_send[k, :, q + e, 0:cols] = logits
        return carry

    lax.fori_loop(0, chunks, outer_step, 0)
    send_logits(chunks - 1)

    trans = down_ref.shape[0]

    def transition_step(k, carry):
        normed = pair_normed[pl.ds(k * 4, 4)].reshape(4 * cols, LANES)
        hidden = jnp.dot(normed, up_ref[...], preferred_element_type=F32)
        front, back = hidden[:, :trans], hidden[:, trans:]
        active = (front / (1.0 + jnp.exp(-front)) * back).astype(BF16)
        update = jnp.dot(active, down_ref[...], preferred_element_type=F32)
        pair = pair_new[pl.ds(k * 4, 4)].astype(F32) + update.reshape(4, cols, LANES)
        out_ref[pl.ds(k * 4, 4)] = pair.astype(BF16)
        return carry

    lax.fori_loop(0, rows // 8, transition_step, 0)

    pieces = weight_buf.shape[1]
    per = heads // pieces

    @pl.when(home == c)
    def _():
        for src in range(C):
            @pl.when(src != c)
            def _():
                for k in range(chunks):
                    pltpu.make_async_remote_copy(
                        src_ref=logit_send.at[k], dst_ref=logit_buf.at[src, k],
                        send_sem=s_logit.at[k], recv_sem=r_logit.at[src, k],
                        device_id=(r, src), device_id_type=MESH).wait_recv()

        lane = lax.broadcasted_iota(jnp.int32, (rows, C * LANES), 1)
        valid = (lane % LANES < cols) & (
            lane // LANES * cols + lane % LANES < length_ref[0])
        for h in range(heads):
            logits = jnp.concatenate(
                [logit_buf[src, :, h].reshape(rows, LANES) for src in range(C)], axis=1)
            logits = jnp.where(valid, logits, MASKED)
            expo = jnp.exp(logits - jnp.max(logits, axis=1, keepdims=True))
            weights = expo / jnp.sum(expo, axis=1, keepdims=True)
            weight_buf[r % ratio, h // per, h % per] = weights.astype(BF16)

        for p in range(pieces):
            for e in range(len(steps)):
                weight_copy(r % ratio, p, e).start()

    lax.fori_loop(rows // 8, rows // 4, transition_step, 0)

    for t in range(1, C):
        wait_norm((c + t) % C)
    for src in range(C):
        for g in range(groups):
            part = jnp.dot(
                normed_buf[src, :, g * group_width:(g + 1) * group_width], value_w_ref[...],
                preferred_element_type=F32).astype(BF16)
            for h in range(heads):
                at = (h * groups + g) * LANES
                values[src * LANES:src * LANES + cols, at:at + LANES] = part[
                    :, h * LANES:(h + 1) * LANES]

    for p in range(pieces):
        for half in range(ratio):
            rel = relation(half)

            @pl.when(rel != 0)
            def _():
                weight_copy(half, p, 0).wait_recv()
                for e, bit in enumerate(steps):
                    @pl.when(rel % (2 * bit) == 0)
                    def _():
                        weight_copy(half, p, e).start()

    span = groups * LANES
    for h in range(heads):
        weights = jnp.concatenate(
            [weight_buf[half, h // per, h % per].astype(F32) for half in range(ratio)],
            axis=0).astype(BF16)
        mean = jnp.dot(weights, values[:, h * span:(h + 1) * span], preferred_element_type=F32)
        mixed = (gates[:, h * span:(h + 1) * span] * mean).astype(BF16)
        for g in range(groups):
            at = (g * heads + h) * LANES
            gated[:, at:at + LANES] = mixed[:, g * LANES:(g + 1) * LANES]
    for g in range(groups):
        part = jnp.dot(
            gated[:, g * heads * LANES:(g + 1) * heads * LANES], final_w_ref[...],
            preferred_element_type=F32)
        sl = slice(g * group_width, (g + 1) * group_width)
        msa_ref[:, sl] = (homolog_ref[:, sl].astype(F32) + part).astype(BF16)

    for t in range(1, R):
        right_copy(t).wait_send()
    for t in range(1, C):
        norm_copy(t).wait_send()
    for h in range(ratio):
        for t in range(C):
            @pl.when(jnp.logical_not((c * ratio + h == r) & (t == 0)))
            def _():
                left_copy(h, t).wait_send()

    @pl.when(home != c)
    def _():
        for k in range(chunks):
            logit_copy(k).wait_send()

    for p in range(pieces):
        for half in range(ratio):
            rel = relation(half)
            for e, bit in enumerate(steps):
                @pl.when(rel % (2 * bit) == 0)
                def _():
                    weight_copy(half, p, e).wait_send()


def local(
    R,
    C,
    homolog_matrix,
    contact_matrix,
    genuine_homolog_total,
    genuine_chain_length,
    tensor_product_matrices,
    tensor_product_final,
    mixing_value_gate_matrix,
    mixing_logit_matrix,
    mixing_final_matrix,
    feedforward_gate_expand,
    feedforward_shrink_matrix,
):
    seqs, cols, feats = homolog_matrix.shape
    rows, _, pair_width = contact_matrix.shape
    ch = tensor_product_matrices.shape[2] // 2
    heads = mixing_logit_matrix.shape[2]
    hidden = mixing_final_matrix.shape[1]
    head_width = hidden // heads
    ratio = R // C
    chunks = rows // 8
    pack = LANES // head_width
    groups = seqs // pack
    r = lax.axis_index("row")
    c = lax.axis_index("col")
    seq_ids = r * seqs + jnp.arange(seqs, dtype=jnp.int32)
    res_ids = c * cols + jnp.arange(cols, dtype=jnp.int32)
    seq_float = (seq_ids < genuine_homolog_total[0]).astype(F32)
    res_float = (res_ids < genuine_chain_length[0]).astype(F32)
    flipped = homolog_matrix.transpose(1, 0, 2)
    normed = standardize_features(homolog_matrix).astype(BF16)
    normed_flat = normed.transpose(1, 0, 2).reshape(cols, seqs * feats)
    left_w = tensor_product_matrices[0][:, :ch]
    right_w = tensor_product_matrices[0][:, ch:]
    right = jnp.einsum("sjf,fd->sdj", normed, right_w, preferred_element_type=F32)
    right = (right * (seq_float[:, None, None] * res_float[None, None, :])).astype(BF16)
    right = jnp.pad(right, ((0, 0), (0, 0), (0, LANES - cols))).reshape(seqs, ch * LANES)
    left = jnp.einsum("sjf,fc->sjc", normed, left_w, preferred_element_type=F32)
    left = (left * (seq_float[:, None, None] * res_float[None, :, None])).astype(BF16)
    left = left.reshape(seqs, ratio, rows * ch).transpose(1, 0, 2)
    outer_w = tensor_product_final[0].reshape(ch, ch, pair_width).transpose(2, 1, 0)
    outer_w = outer_w.reshape(pair_width, ch * ch)
    same = jnp.eye(pack, dtype=BF16)
    vg = mixing_value_gate_matrix[0].reshape(feats, 2, heads, head_width)
    spread = vg[None, :, :, :, None, :] * same[:, None, None, None, :, None]
    spread = spread.reshape(pack * feats, 2, heads * LANES)
    final = mixing_final_matrix[0].reshape(heads, 1, head_width, 1, feats)
    final = (final * same[None, :, None, :, None]).reshape(heads * LANES, pack * feats)
    dims = (R, C, ratio, rows, cols, seqs * feats, heads, chunks)
    vmem = pl.BlockSpec(memory_space=pltpu.VMEM)
    smem = pl.BlockSpec(memory_space=pltpu.SMEM)
    dma = pltpu.SemaphoreType.DMA
    msa, pair_out = pl.pallas_call(
        functools.partial(kernel, dims),
        out_shape=(
            jax.ShapeDtypeStruct((cols, seqs * feats), BF16),
            jax.ShapeDtypeStruct(contact_matrix.shape, BF16),
        ),
        in_specs=[smem] * 2 + [vmem] * 12,
        out_specs=(vmem, vmem),
        scratch_shapes=[
            pltpu.VMEM((R, seqs, ch * LANES), BF16),
            pltpu.VMEM((R, seqs, rows * ch), BF16),
            pltpu.VMEM((C, cols, seqs * feats), BF16),
            pltpu.VMEM((chunks, heads, 8, LANES), F32),
            pltpu.VMEM((C, chunks, heads, 8, LANES), F32),
            pltpu.VMEM((ratio, heads // 2, 2, rows, C * LANES), BF16),
            pltpu.VMEM((R * seqs, ch * LANES), BF16),
            pltpu.VMEM((rows * ch, R * seqs), BF16),
            pltpu.VMEM((8, ch * ch, LANES), BF16),
            pltpu.VMEM((rows, cols, pair_width), BF16),
            pltpu.VMEM((rows, cols, pair_width), BF16),
            pltpu.VMEM((C * LANES, heads * groups * LANES), BF16),
            pltpu.VMEM((cols, heads * groups * LANES), F32),
            pltpu.VMEM((cols, heads * groups * LANES), BF16),
            dma((R,)), dma((R,)), dma((ratio, C)), dma((R,)), dma((C,)), dma((C,)),
            dma((chunks,)), dma((C, chunks)),
            dma((ratio, heads // 2, R.bit_length())), dma((ratio, heads // 2)),
        ],
        compiler_params=pltpu.CompilerParams(
            collective_id=0, has_side_effects=True, vmem_limit_bytes=60 * 1024 * 1024
        ),
        name="msa_block",
    )(
        genuine_homolog_total, genuine_chain_length,
        right, left, normed_flat, flipped.reshape(cols, seqs * feats), contact_matrix,
        outer_w, spread[:, 0], spread[:, 1], mixing_logit_matrix[0].T, final,
        feedforward_gate_expand[0], feedforward_shrink_matrix[0],
    )
    return (msa.reshape(cols, seqs, feats).transpose(1, 0, 2), pair_out)


def solution(mesh):
    in_specs = (P("row", "col", None), P("row", "col", None)) + (P(),) * 9
    out_specs = (P("row", "col", None), P("row", "col", None))
    body = functools.partial(local, mesh.shape["row"], mesh.shape["col"])
    return jax.shard_map(body, mesh=mesh, in_specs=in_specs, out_specs=out_specs, check_vma=False)
```

```python
import functools

import jax
import jax.numpy as jnp
from jax import lax
from jax.experimental import pallas as pl
from jax.experimental.pallas import tpu as pltpu
from jax.sharding import PartitionSpec as P

EPSILON = 1e-05
MASKED = -1000000000.0
MESH = pl.DeviceIdType.MESH
LANES = 128
BF16 = jnp.bfloat16
F32 = jnp.float32


def standardize_features(field):
    field = field.astype(F32)
    center = field - jnp.mean(field, axis=-1, keepdims=True)
    spread = jnp.mean(center * center, axis=-1, keepdims=True)
    return center * lax.rsqrt(spread + EPSILON)


def flip(index, mask):
    bit = 1
    while bit <= mask:
        if mask & bit:
            index = index + bit - 2 * bit * ((index // bit) % 2)
        bit *= 2
    return index


def kernel(
    dims,
    seqs_ref, length_ref,
    right_ref, left_ref, normed_ref, homolog_ref, pair_ref,
    outer_w_ref, value_w_ref, gate_w_ref, logit_w_ref, final_w_ref, up_ref, down_ref,
    msa_ref, out_ref,
    right_buf, left_buf, normed_buf, logit_send, logit_buf, stat_send, stat_buf, expo_tile,
    right_all, left_all, product, pair_new, pair_normed, values, gates, gated,
    s_right, r_right, s_left, r_left, s_norm, r_norm, s_logit, r_logit, s_stat, r_stat,
):
    R, C, ratio, rows, cols, width, heads, chunks = dims
    r = lax.axis_index("row")
    c = lax.axis_index("col")
    home = r // ratio

    barrier = pltpu.get_barrier_semaphore()

    def greet(row, col):
        pl.semaphore_signal(barrier, inc=1, device_id=(row, col), device_id_type=MESH)

    for t in range(1, R):
        greet((r + t) % R, c)
    for t in range(1, C):
        greet(r, (c + t) % C)
    for t in range(R):
        row = (r + t) % R

        @pl.when(jnp.logical_not((row == r) & (home == c)))
        def _():
            greet(row, home)

    for h in range(ratio):
        for t in range(C):
            row, col = c * ratio + h, (c + t) % C

            @pl.when(jnp.logical_not((row == r) & (col == c)))
            def _():
                greet(row, col)

    own = jnp.where(home == c, 1, 0)
    pl.semaphore_wait(barrier, (R - 1) + (C - 1) + 2 * R - 2 * own)

    def right_copy(n):
        root = flip(r, n & (n - 1))
        return pltpu.make_async_remote_copy(
            src_ref=right_buf.at[root] if n & (n - 1) else right_ref,
            dst_ref=right_buf.at[root],
            send_sem=s_right.at[n], recv_sem=r_right.at[n],
            device_id=(flip(r, n & -n), c), device_id_type=MESH)

    def left_copy(h, t):
        return pltpu.make_async_remote_copy(
            src_ref=left_ref.at[h], dst_ref=left_buf.at[r],
            send_sem=s_left.at[h, t], recv_sem=r_left.at[r],
            device_id=(c * ratio + h, (c + t) % C), device_id_type=MESH)

    def norm_copy(t):
        return pltpu.make_async_remote_copy(
            src_ref=normed_ref, dst_ref=normed_buf.at[c],
            send_sem=s_norm.at[t], recv_sem=r_norm.at[c],
            device_id=(r, (c + t) % C), device_id_type=MESH)

    def logit_copy(k, t):
        return pltpu.make_async_remote_copy(
            src_ref=logit_send.at[k], dst_ref=logit_buf.at[r % ratio, c, k],
            send_sem=s_logit.at[k, t], recv_sem=r_logit.at[r % ratio, c, k],
            device_id=((r + t) % R, home), device_id_type=MESH)

    def stat_copy(t):
        return pltpu.make_async_remote_copy(
            src_ref=stat_send, dst_ref=stat_buf.at[r % ratio, c],
            send_sem=s_stat.at[t], recv_sem=r_stat.at[r % ratio, c],
            device_id=((r + t) % R, home), device_id_type=MESH)

    for h in range(ratio):
        for t in range(C):
            mine = (c * ratio + h == r) & (t == 0)

            @pl.when(jnp.logical_not(mine))
            def _():
                left_copy(h, t).start()

            @pl.when(mine)
            def _():
                left_buf[r] = left_ref[h]

    steps = [R >> (e + 1) for e in range(R.bit_length() - 1)]
    for bit in steps:
        right_copy(bit).start()
    right_buf[r] = right_ref[...]
    normed_buf[c] = normed_ref[...]

    def wait_left(src):
        pltpu.make_async_remote_copy(
            src_ref=left_ref.at[0], dst_ref=left_buf.at[src],
            send_sem=s_left.at[0, 0], recv_sem=r_left.at[src],
            device_id=(src, home), device_id_type=MESH).wait_recv()

    def wait_right(n):
        pltpu.make_async_remote_copy(
            src_ref=right_ref, dst_ref=right_buf.at[flip(r, n)],
            send_sem=s_right.at[n], recv_sem=r_right.at[n],
            device_id=(flip(r, n & -n), c), device_id_type=MESH).wait_recv()

    def wait_norm(src):
        pltpu.make_async_remote_copy(
            src_ref=normed_ref, dst_ref=normed_buf.at[src],
            send_sem=s_norm.at[0], recv_sem=r_norm.at[src],
            device_id=(r, src), device_id_type=MESH).wait_recv()

    for n in sorted(range(1, R), key=lambda n: (bin(n).count("1"), -(n & -n))):
        wait_right(n)
        for bit in steps:
            if bit < n & -n:
                right_copy(n + bit).start()

    for t in range(1, C):
        norm_copy(t).start()

    groups = gates.shape[1] // (heads * LANES)
    group_width = width // groups
    for g in range(groups):
        part = jnp.dot(
            normed_ref[:, g * group_width:(g + 1) * group_width], gate_w_ref[...],
            preferred_element_type=F32)
        for h in range(heads):
            at = (h * groups + g) * LANES
            gates[:, at:at + LANES] = jax.nn.sigmoid(part[:, h * LANES:(h + 1) * LANES])
    values[...] = jnp.zeros_like(values)
    stat_send[...] = jnp.zeros_like(stat_send)

    for src in range(R):
        @pl.when(jnp.logical_not((src == r) & (home == c)))
        def _():
            wait_left(src)

    left_t = left_buf[...].astype(F32).reshape(R * left_buf.shape[1], left_buf.shape[2]).T
    left_all[...] = left_t.astype(BF16)
    right_flat = right_buf[...].astype(F32).reshape(right_all.shape[0], right_buf.shape[2])
    zeros = jnp.zeros((right_all.shape[0], LANES - cols), F32)
    for d in range(right_buf.shape[2] // cols):
        right_all[:, d * LANES:(d + 1) * LANES] = jnp.concatenate(
            [right_flat[:, d * cols:(d + 1) * cols], zeros], axis=1).astype(BF16)

    inverse = 1.0 / jnp.maximum(seqs_ref[0].astype(F32), 1.0)
    ch = product.shape[1] // (right_all.shape[1] // LANES)

    def send_logits(k):
        for t in range(R):
            if t > 0:
                logit_copy(k, t).start()
            else:
                @pl.when(home == c)
                def _():
                    logit_buf[r % ratio, c, k] = logit_send[k]

                @pl.when(home != c)
                def _():
                    logit_copy(k, 0).start()

    row_lane = lax.broadcasted_iota(jnp.int32, (heads, LANES), 1)
    real = c * cols + lax.broadcasted_iota(jnp.int32, (heads, cols), 1) < length_ref[0]

    def outer_step(k, carry):
        @pl.when(k > 0)
        def _():
            send_logits(k - 1)

        lhs = left_all[pl.ds(pl.multiple_of(k * 8 * ch, 8 * ch), 8 * ch), :]
        for d in range(0, right_all.shape[1] // LANES, 2):
            p = jnp.dot(lhs, right_all[:, d * LANES:(d + 2) * LANES], preferred_element_type=F32)
            p = (p * inverse).astype(BF16)
            for e in range(2):
                product[:, (d + e) * ch:(d + e + 1) * ch, :] = p[
                    :, e * LANES:(e + 1) * LANES].reshape(8, ch, LANES)
        for q in range(0, 8, 2):
            both = jnp.concatenate([product[q], product[q + 1]], axis=1)
            update = jnp.dot(outer_w_ref[...], both, preferred_element_type=F32)
            for e in range(2):
                i = k * 8 + q + e
                step = update[:, e * LANES:(e + 1) * LANES].T[:cols]
                pair = (pair_ref[i].astype(F32) + step).astype(BF16)
                pair_new[i] = pair
                normed = standardize_features(pair).astype(BF16)
                pair_normed[i] = normed
                logits = lax.dot_general(
                    logit_w_ref[...], normed, (((1,), (1,)), ((), ())),
                    preferred_element_type=F32)
                logits = jnp.where(real, logits, MASKED)
                peak = jnp.max(logits, axis=1, keepdims=True)
                expo = jnp.exp(logits - peak)
                expo_tile[:, q + e, 0:cols] = expo
                stat_send[0] = jnp.where(row_lane == i, peak, stat_send[0])
                stat_send[1] = jnp.where(
                    row_lane == i, jnp.sum(expo, axis=1, keepdims=True), stat_send[1])
        logit_send[k] = jnp.concatenate(
            [expo_tile[h, :, 0:cols] for h in range(heads)], axis=1).astype(BF16)
        return carry

    lax.fori_loop(0, chunks, outer_step, 0)
    send_logits(chunks - 1)
    for t in range(R):
        if t > 0:
            stat_copy(t).start()
        else:
            @pl.when(home == c)
            def _():
                stat_buf[r % ratio, c] = stat_send[...]

            @pl.when(home != c)
            def _():
                stat_copy(0).start()

    trans = down_ref.shape[0]

    def transition_step(k, carry):
        normed = pair_normed[pl.ds(k * 4, 4)].reshape(4 * cols, LANES)
        hidden = jnp.dot(normed, up_ref[...], preferred_element_type=F32)
        front, back = hidden[:, :trans], hidden[:, trans:]
        active = (front / (1.0 + jnp.exp(-front)) * back).astype(BF16)
        update = jnp.dot(active, down_ref[...], preferred_element_type=F32)
        pair = pair_new[pl.ds(k * 4, 4)].astype(F32) + update.reshape(4, cols, LANES)
        out_ref[pl.ds(k * 4, 4)] = pair.astype(BF16)
        return carry

    lax.fori_loop(0, rows // 4, transition_step, 0)

    for t in range(1, C):
        wait_norm((c + t) % C)
    for src in range(C):
        for g in range(groups):
            part = jnp.dot(
                normed_buf[src, :, g * group_width:(g + 1) * group_width], value_w_ref[...],
                preferred_element_type=F32).astype(BF16)
            for h in range(heads):
                at = (h * groups + g) * LANES
                values[src * LANES:src * LANES + cols, at:at + LANES] = part[
                    :, h * LANES:(h + 1) * LANES]

    for h in range(ratio):
        for src in range(C):
            @pl.when(jnp.logical_not((c * ratio + h == r) & (src == c)))
            def _():
                for k in range(chunks):
                    pltpu.make_async_remote_copy(
                        src_ref=logit_send.at[k], dst_ref=logit_buf.at[h, src, k],
                        send_sem=s_logit.at[k, 0], recv_sem=r_logit.at[h, src, k],
                        device_id=(r, home), device_id_type=MESH).wait_recv()
                pltpu.make_async_remote_copy(
                    src_ref=stat_send, dst_ref=stat_buf.at[h, src],
                    send_sem=s_stat.at[0], recv_sem=r_stat.at[h, src],
                    device_id=(r, home), device_id_type=MESH).wait_recv()

    scales = []
    for half in range(ratio):
        peaks = [stat_buf[half, src, 0] for src in range(C)]
        top = functools.reduce(jnp.maximum, peaks)
        shifts = [jnp.exp(peak - top) for peak in peaks]
        total = sum(shift * stat_buf[half, src, 1] for src, shift in enumerate(shifts))
        total = jnp.where(row_lane < rows, total, 1.0)
        scales.append([(shift / total).T for shift in shifts])
    gap = jnp.zeros((rows, LANES - cols), F32)
    expos = [[logit_buf[half, src].astype(F32).reshape(rows, heads * cols) for src in range(C)]
             for half in range(ratio)]
    span = groups * LANES
    for h in range(heads):
        weights = jnp.concatenate([
            jnp.concatenate([
                piece for src in range(C) for piece in (
                    expos[half][src][:, h * cols:(h + 1) * cols]
                    * scales[half][src][:rows, h:h + 1], gap)], axis=1)
            for half in range(ratio)], axis=0).astype(BF16)
        mean = jnp.dot(weights, values[:, h * span:(h + 1) * span], preferred_element_type=F32)
        mixed = (gates[:, h * span:(h + 1) * span] * mean).astype(BF16)
        for g in range(groups):
            at = (g * heads + h) * LANES
            gated[:, at:at + LANES] = mixed[:, g * LANES:(g + 1) * LANES]
    for g in range(groups):
        part = jnp.dot(
            gated[:, g * heads * LANES:(g + 1) * heads * LANES], final_w_ref[...],
            preferred_element_type=F32)
        sl = slice(g * group_width, (g + 1) * group_width)
        msa_ref[:, sl] = (homolog_ref[:, sl].astype(F32) + part).astype(BF16)

    for t in range(1, R):
        right_copy(t).wait_send()
    for t in range(1, C):
        norm_copy(t).wait_send()
    for h in range(ratio):
        for t in range(C):
            @pl.when(jnp.logical_not((c * ratio + h == r) & (t == 0)))
            def _():
                left_copy(h, t).wait_send()

    def finish(k, carry):
        for t in range(1, R):
            logit_copy(k, t).wait_send()

        @pl.when(home != c)
        def _():
            logit_copy(k, 0).wait_send()

        return carry

    for t in range(1, R):
        stat_copy(t).wait_send()

    @pl.when(home != c)
    def _():
        stat_copy(0).wait_send()

    lax.fori_loop(0, chunks, finish, 0)


def local(
    R,
    C,
    homolog_matrix,
    contact_matrix,
    genuine_homolog_total,
    genuine_chain_length,
    tensor_product_matrices,
    tensor_product_final,
    mixing_value_gate_matrix,
    mixing_logit_matrix,
    mixing_final_matrix,
    feedforward_gate_expand,
    feedforward_shrink_matrix,
):
    seqs, cols, feats = homolog_matrix.shape
    rows, _, pair_width = contact_matrix.shape
    ch = tensor_product_matrices.shape[2] // 2
    heads = mixing_logit_matrix.shape[2]
    hidden = mixing_final_matrix.shape[1]
    head_width = hidden // heads
    ratio = R // C
    chunks = rows // 8
    pack = LANES // head_width
    groups = seqs // pack
    r = lax.axis_index("row")
    c = lax.axis_index("col")
    seq_ids = r * seqs + jnp.arange(seqs, dtype=jnp.int32)
    res_ids = c * cols + jnp.arange(cols, dtype=jnp.int32)
    seq_float = (seq_ids < genuine_homolog_total[0]).astype(F32)
    res_float = (res_ids < genuine_chain_length[0]).astype(F32)
    flipped = homolog_matrix.transpose(1, 0, 2)
    normed = standardize_features(homolog_matrix).astype(BF16)
    normed_flat = normed.transpose(1, 0, 2).reshape(cols, seqs * feats)
    left_w = tensor_product_matrices[0][:, :ch]
    right_w = tensor_product_matrices[0][:, ch:]
    right = jnp.einsum("sjf,fd->sdj", normed, right_w, preferred_element_type=F32)
    right = (right * (seq_float[:, None, None] * res_float[None, None, :])).astype(BF16)
    right = right.reshape(seqs, ch * cols)
    left = jnp.einsum("sjf,fc->sjc", normed, left_w, preferred_element_type=F32)
    left = (left * (seq_float[:, None, None] * res_float[None, :, None])).astype(BF16)
    left = left.reshape(seqs, ratio, rows * ch).transpose(1, 0, 2)
    outer_w = tensor_product_final[0].reshape(ch, ch, pair_width).transpose(2, 1, 0)
    outer_w = outer_w.reshape(pair_width, ch * ch)
    same = jnp.eye(pack, dtype=BF16)
    vg = mixing_value_gate_matrix[0].reshape(feats, 2, heads, head_width)
    spread = vg[None, :, :, :, None, :] * same[:, None, None, None, :, None]
    spread = spread.reshape(pack * feats, 2, heads * LANES)
    final = mixing_final_matrix[0].reshape(heads, 1, head_width, 1, feats)
    final = (final * same[None, :, None, :, None]).reshape(heads * LANES, pack * feats)
    dims = (R, C, ratio, rows, cols, seqs * feats, heads, chunks)
    vmem = pl.BlockSpec(memory_space=pltpu.VMEM)
    smem = pl.BlockSpec(memory_space=pltpu.SMEM)
    dma = pltpu.SemaphoreType.DMA
    msa, pair_out = pl.pallas_call(
        functools.partial(kernel, dims),
        out_shape=(
            jax.ShapeDtypeStruct((cols, seqs * feats), BF16),
            jax.ShapeDtypeStruct(contact_matrix.shape, BF16),
        ),
        in_specs=[smem] * 2 + [vmem] * 12,
        out_specs=(vmem, vmem),
        scratch_shapes=[
            pltpu.VMEM((R, seqs, ch * cols), BF16),
            pltpu.VMEM((R, seqs, rows * ch), BF16),
            pltpu.VMEM((C, cols, seqs * feats), BF16),
            pltpu.VMEM((chunks, 8, heads * cols), BF16),
            pltpu.VMEM((ratio, C, chunks, 8, heads * cols), BF16),
            pltpu.VMEM((2, heads, LANES), F32),
            pltpu.VMEM((ratio, C, 2, heads, LANES), F32),
            pltpu.VMEM((heads, 8, LANES), F32),
            pltpu.VMEM((R * seqs, ch * LANES), BF16),
            pltpu.VMEM((rows * ch, R * seqs), BF16),
            pltpu.VMEM((8, ch * ch, LANES), BF16),
            pltpu.VMEM((rows, cols, pair_width), BF16),
            pltpu.VMEM((rows, cols, pair_width), BF16),
            pltpu.VMEM((C * LANES, heads * groups * LANES), BF16),
            pltpu.VMEM((cols, heads * groups * LANES), F32),
            pltpu.VMEM((cols, heads * groups * LANES), BF16),
            dma((R,)), dma((R,)), dma((ratio, C)), dma((R,)), dma((C,)), dma((C,)),
            dma((chunks, R)), dma((ratio, C, chunks)), dma((R,)), dma((ratio, C)),
        ],
        compiler_params=pltpu.CompilerParams(
            collective_id=0, has_side_effects=True, vmem_limit_bytes=60 * 1024 * 1024
        ),
        name="msa_block",
    )(
        genuine_homolog_total, genuine_chain_length,
        right, left, normed_flat, flipped.reshape(cols, seqs * feats), contact_matrix,
        outer_w, spread[:, 0], spread[:, 1], mixing_logit_matrix[0].T, final,
        feedforward_gate_expand[0], feedforward_shrink_matrix[0],
    )
    return (msa.reshape(cols, seqs, feats).transpose(1, 0, 2), pair_out)


def solution(mesh):
    in_specs = (P("row", "col", None), P("row", "col", None)) + (P(),) * 9
    out_specs = (P("row", "col", None), P("row", "col", None))
    body = functools.partial(local, mesh.shape["row"], mesh.shape["col"])
    return jax.shard_map(body, mesh=mesh, in_specs=in_specs, out_specs=out_specs, check_vma=False)
```

```python
import functools

import jax
import jax.numpy as jnp
from jax import lax
from jax.experimental import pallas as pl
from jax.experimental.pallas import tpu as pltpu
from jax.sharding import PartitionSpec as P

EPSILON = 1e-05
MASKED = -1000000000.0
MESH = pl.DeviceIdType.MESH
LANES = 128
BF16 = jnp.bfloat16
F32 = jnp.float32


def standardize_features(field):
    field = field.astype(F32)
    center = field - jnp.mean(field, axis=-1, keepdims=True)
    spread = jnp.mean(center * center, axis=-1, keepdims=True)
    return center * lax.rsqrt(spread + EPSILON)


def flip(index, mask):
    bit = 1
    while bit <= mask:
        if mask & bit:
            index = index + bit - 2 * bit * ((index // bit) % 2)
        bit *= 2
    return index


def kernel(
    dims,
    seqs_ref, length_ref,
    right_ref, left_ref, normed_ref, homolog_ref, pair_ref,
    outer_w_ref, mix_ref, logit_w_ref, mix_out_ref, up_ref, down_ref,
    msa_ref, out_ref,
    right_buf, left_buf, normed_buf, logit_send, logit_buf, stat_send, stat_buf, expo_tile,
    right_all, left_all, product, pair_new, pair_normed, values, gates, gated,
    value_w_ref, gate_w_ref, final_w_ref,
    s_right, r_right, s_left, r_left, s_norm, r_norm, s_logit, r_logit, s_stat, r_stat,
):
    R, C, ratio, rows, cols, width, heads, chunks = dims
    r = lax.axis_index("row")
    c = lax.axis_index("col")
    home = r // ratio

    barrier = pltpu.get_barrier_semaphore()

    def greet(row, col):
        pl.semaphore_signal(barrier, inc=1, device_id=(row, col), device_id_type=MESH)

    for t in range(1, R):
        greet((r + t) % R, c)
    for t in range(1, C):
        greet(r, (c + t) % C)
    for t in range(R):
        row = (r + t) % R

        @pl.when(jnp.logical_not((row == r) & (home == c)))
        def _():
            greet(row, home)

    for h in range(ratio):
        for t in range(C):
            row, col = c * ratio + h, (c + t) % C

            @pl.when(jnp.logical_not((row == r) & (col == c)))
            def _():
                greet(row, col)

    own = jnp.where(home == c, 1, 0)
    pl.semaphore_wait(barrier, (R - 1) + (C - 1) + 2 * R - 2 * own)

    def right_copy(n):
        root = flip(r, n & (n - 1))
        return pltpu.make_async_remote_copy(
            src_ref=right_buf.at[root] if n & (n - 1) else right_ref,
            dst_ref=right_buf.at[root],
            send_sem=s_right.at[n], recv_sem=r_right.at[n],
            device_id=(flip(r, n & -n), c), device_id_type=MESH)

    def left_copy(h, t):
        return pltpu.make_async_remote_copy(
            src_ref=left_ref.at[h], dst_ref=left_buf.at[r],
            send_sem=s_left.at[h, t], recv_sem=r_left.at[r],
            device_id=(c * ratio + h, (c + t) % C), device_id_type=MESH)

    def norm_copy(t):
        return pltpu.make_async_remote_copy(
            src_ref=normed_ref, dst_ref=normed_buf.at[c],
            send_sem=s_norm.at[t], recv_sem=r_norm.at[c],
            device_id=(r, (c + t) % C), device_id_type=MESH)

    def logit_copy(k, t):
        return pltpu.make_async_remote_copy(
            src_ref=logit_send.at[k], dst_ref=logit_buf.at[r % ratio, c, k],
            send_sem=s_logit.at[k, t], recv_sem=r_logit.at[r % ratio, c, k],
            device_id=((r + t) % R, home), device_id_type=MESH)

    def stat_copy(t):
        return pltpu.make_async_remote_copy(
            src_ref=stat_send, dst_ref=stat_buf.at[r % ratio, c],
            send_sem=s_stat.at[t], recv_sem=r_stat.at[r % ratio, c],
            device_id=((r + t) % R, home), device_id_type=MESH)

    for h in range(ratio):
        for t in range(C):
            mine = (c * ratio + h == r) & (t == 0)

            @pl.when(jnp.logical_not(mine))
            def _():
                left_copy(h, t).start()

            @pl.when(mine)
            def _():
                left_buf[r] = left_ref[h]

    steps = [R >> (e + 1) for e in range(R.bit_length() - 1)]
    for bit in steps:
        right_copy(bit).start()
    right_buf[r] = right_ref[...]
    normed_buf[c] = normed_ref[...]

    def wait_left(src):
        pltpu.make_async_remote_copy(
            src_ref=left_ref.at[0], dst_ref=left_buf.at[src],
            send_sem=s_left.at[0, 0], recv_sem=r_left.at[src],
            device_id=(src, home), device_id_type=MESH).wait_recv()

    def wait_right(n):
        pltpu.make_async_remote_copy(
            src_ref=right_ref, dst_ref=right_buf.at[flip(r, n)],
            send_sem=s_right.at[n], recv_sem=r_right.at[n],
            device_id=(flip(r, n & -n), c), device_id_type=MESH).wait_recv()

    def wait_norm(src):
        pltpu.make_async_remote_copy(
            src_ref=normed_ref, dst_ref=normed_buf.at[src],
            send_sem=s_norm.at[0], recv_sem=r_norm.at[src],
            device_id=(r, src), device_id_type=MESH).wait_recv()

    feats, hidden_width = mix_out_ref.shape
    head_width = hidden_width // heads
    pack = LANES // head_width
    shape = (pack * feats, feats)
    stack = (lax.broadcasted_iota(jnp.int32, shape, 0) % feats
             == lax.broadcasted_iota(jnp.int32, shape, 1)).astype(F32).astype(BF16)
    shape = (hidden_width, heads * LANES)
    row, lane = (lax.broadcasted_iota(jnp.int32, shape, axis) for axis in (0, 1))
    widen = ((row // head_width == lane // LANES) & (row % head_width == lane % head_width))
    widen = widen.astype(F32).astype(BF16)
    shape = (pack * feats, heads * LANES)
    row, lane = (lax.broadcasted_iota(jnp.int32, shape, axis) for axis in (0, 1))
    diagonal = row // feats == lane % LANES // head_width
    for source, target in (
        (mix_ref[:, :hidden_width], value_w_ref),
        (mix_ref[:, hidden_width:], gate_w_ref),
        (mix_out_ref[...], final_w_ref),
    ):
        tall = jnp.dot(stack, source, preferred_element_type=F32).astype(BF16)
        wide = jnp.dot(tall, widen, preferred_element_type=F32)
        target[...] = jnp.where(diagonal, wide, 0.0).astype(BF16)

    for n in sorted(range(1, R), key=lambda n: (bin(n).count("1"), -(n & -n))):
        wait_right(n)
        for bit in steps:
            if bit < n & -n:
                right_copy(n + bit).start()

    for t in range(1, C):
        norm_copy(t).start()

    groups = gates.shape[1] // (heads * LANES)
    group_width = width // groups
    for g in range(groups):
        part = jnp.dot(
            normed_ref[:, g * group_width:(g + 1) * group_width], gate_w_ref[...],
            preferred_element_type=F32)
        for h in range(heads):
            at = (h * groups + g) * LANES
            gates[:, at:at + LANES] = jax.nn.sigmoid(part[:, h * LANES:(h + 1) * LANES])
    values[...] = jnp.zeros_like(values)
    stat_send[...] = jnp.zeros_like(stat_send)

    for src in range(R):
        @pl.when(jnp.logical_not((src == r) & (home == c)))
        def _():
            wait_left(src)

    left_t = left_buf[...].astype(F32).reshape(R * left_buf.shape[1], left_buf.shape[2]).T
    left_all[...] = left_t.astype(BF16)
    right_flat = right_buf[...].astype(F32).reshape(right_all.shape[0], right_buf.shape[2])
    zeros = jnp.zeros((right_all.shape[0], LANES - cols), F32)
    for d in range(right_buf.shape[2] // cols):
        right_all[:, d * LANES:(d + 1) * LANES] = jnp.concatenate(
            [right_flat[:, d * cols:(d + 1) * cols], zeros], axis=1).astype(BF16)

    inverse = 1.0 / jnp.maximum(seqs_ref[0].astype(F32), 1.0)
    ch = product.shape[1] // (right_all.shape[1] // LANES)

    def send_logits(k):
        for t in range(R):
            if t > 0:
                logit_copy(k, t).start()
            else:
                @pl.when(home == c)
                def _():
                    logit_buf[r % ratio, c, k] = logit_send[k]

                @pl.when(home != c)
                def _():
                    logit_copy(k, 0).start()

    row_lane = lax.broadcasted_iota(jnp.int32, (heads, LANES), 1)
    real = c * cols + lax.broadcasted_iota(jnp.int32, (heads, cols), 1) < length_ref[0]

    def outer_step(k, carry):
        @pl.when(k > 0)
        def _():
            send_logits(k - 1)

        lhs = left_all[pl.ds(pl.multiple_of(k * 8 * ch, 8 * ch), 8 * ch), :]
        for d in range(0, right_all.shape[1] // LANES, 2):
            p = jnp.dot(lhs, right_all[:, d * LANES:(d + 2) * LANES], preferred_element_type=F32)
            p = (p * inverse).astype(BF16)
            for e in range(2):
                product[:, (d + e) * ch:(d + e + 1) * ch, :] = p[
                    :, e * LANES:(e + 1) * LANES].reshape(8, ch, LANES)
        for q in range(0, 8, 2):
            both = jnp.concatenate([product[q], product[q + 1]], axis=1)
            update = jnp.dot(outer_w_ref[...], both, preferred_element_type=F32)
            for e in range(2):
                i = k * 8 + q + e
                step = update[:, e * LANES:(e + 1) * LANES].T[:cols]
                pair = (pair_ref[i].astype(F32) + step).astype(BF16)
                pair_new[i] = pair
                normed = standardize_features(pair).astype(BF16)
                pair_normed[i] = normed
                logits = lax.dot_general(
                    logit_w_ref[...], normed, (((1,), (1,)), ((), ())),
                    preferred_element_type=F32)
                logits = jnp.where(real, logits, MASKED)
                peak = jnp.max(logits, axis=1, keepdims=True)
                expo = jnp.exp(logits - peak)
                expo_tile[:, q + e, 0:cols] = expo
                stat_send[0] = jnp.where(row_lane == i, peak, stat_send[0])
                stat_send[1] = jnp.where(
                    row_lane == i, jnp.sum(expo, axis=1, keepdims=True), stat_send[1])
        logit_send[k] = jnp.concatenate(
            [expo_tile[h, :, 0:cols] for h in range(heads)], axis=1).astype(BF16)
        return carry

    lax.fori_loop(0, chunks, outer_step, 0)
    send_logits(chunks - 1)
    for t in range(R):
        if t > 0:
            stat_copy(t).start()
        else:
            @pl.when(home == c)
            def _():
                stat_buf[r % ratio, c] = stat_send[...]

            @pl.when(home != c)
            def _():
                stat_copy(0).start()

    trans = down_ref.shape[0]

    def transition_step(k, carry):
        normed = pair_normed[pl.ds(k * 4, 4)].reshape(4 * cols, LANES)
        hidden = jnp.dot(normed, up_ref[...], preferred_element_type=F32)
        front, back = hidden[:, :trans], hidden[:, trans:]
        active = (front / (1.0 + jnp.exp(-front)) * back).astype(BF16)
        update = jnp.dot(active, down_ref[...], preferred_element_type=F32)
        pair = pair_new[pl.ds(k * 4, 4)].astype(F32) + update.reshape(4, cols, LANES)
        out_ref[pl.ds(k * 4, 4)] = pair.astype(BF16)
        return carry

    lax.fori_loop(0, rows // 4, transition_step, 0)

    for t in range(1, C):
        wait_norm((c + t) % C)
    for src in range(C):
        for g in range(groups):
            part = jnp.dot(
                normed_buf[src, :, g * group_width:(g + 1) * group_width], value_w_ref[...],
                preferred_element_type=F32).astype(BF16)
            for h in range(heads):
                at = (h * groups + g) * LANES
                values[src * LANES:src * LANES + cols, at:at + LANES] = part[
                    :, h * LANES:(h + 1) * LANES]

    for h in range(ratio):
        for src in range(C):
            @pl.when(jnp.logical_not((c * ratio + h == r) & (src == c)))
            def _():
                for k in range(chunks):
                    pltpu.make_async_remote_copy(
                        src_ref=logit_send.at[k], dst_ref=logit_buf.at[h, src, k],
                        send_sem=s_logit.at[k, 0], recv_sem=r_logit.at[h, src, k],
                        device_id=(r, home), device_id_type=MESH).wait_recv()
                pltpu.make_async_remote_copy(
                    src_ref=stat_send, dst_ref=stat_buf.at[h, src],
                    send_sem=s_stat.at[0], recv_sem=r_stat.at[h, src],
                    device_id=(r, home), device_id_type=MESH).wait_recv()

    scales = []
    for half in range(ratio):
        peaks = [stat_buf[half, src, 0] for src in range(C)]
        top = functools.reduce(jnp.maximum, peaks)
        shifts = [jnp.exp(peak - top) for peak in peaks]
        total = sum(shift * stat_buf[half, src, 1] for src, shift in enumerate(shifts))
        total = jnp.where(row_lane < rows, total, 1.0)
        scales.append([(shift / total).T for shift in shifts])
    gap = jnp.zeros((rows, LANES - cols), F32)
    expos = [[logit_buf[half, src].astype(F32).reshape(rows, heads * cols) for src in range(C)]
             for half in range(ratio)]
    span = groups * LANES
    for h in range(heads):
        weights = jnp.concatenate([
            jnp.concatenate([
                piece for src in range(C) for piece in (
                    expos[half][src][:, h * cols:(h + 1) * cols]
                    * scales[half][src][:rows, h:h + 1], gap)], axis=1)
            for half in range(ratio)], axis=0).astype(BF16)
        mean = jnp.dot(weights, values[:, h * span:(h + 1) * span], preferred_element_type=F32)
        mixed = (gates[:, h * span:(h + 1) * span] * mean).astype(BF16)
        for g in range(groups):
            at = (g * heads + h) * LANES
            gated[:, at:at + LANES] = mixed[:, g * LANES:(g + 1) * LANES]
    for g in range(groups):
        part = lax.dot_general(
            gated[:, g * heads * LANES:(g + 1) * heads * LANES], final_w_ref[...],
            (((1,), (1,)), ((), ())), preferred_element_type=F32)
        sl = slice(g * pack, (g + 1) * pack)
        msa_ref[sl] = (
            homolog_ref[sl].astype(F32) + part.T.reshape(pack, feats, cols)).astype(BF16)

    for t in range(1, R):
        right_copy(t).wait_send()
    for t in range(1, C):
        norm_copy(t).wait_send()
    for h in range(ratio):
        for t in range(C):
            @pl.when(jnp.logical_not((c * ratio + h == r) & (t == 0)))
            def _():
                left_copy(h, t).wait_send()

    def finish(k, carry):
        for t in range(1, R):
            logit_copy(k, t).wait_send()

        @pl.when(home != c)
        def _():
            logit_copy(k, 0).wait_send()

        return carry

    for t in range(1, R):
        stat_copy(t).wait_send()

    @pl.when(home != c)
    def _():
        stat_copy(0).wait_send()

    lax.fori_loop(0, chunks, finish, 0)


def local(
    R,
    C,
    homolog_matrix,
    contact_matrix,
    genuine_homolog_total,
    genuine_chain_length,
    tensor_product_matrices,
    tensor_product_final,
    mixing_value_gate_matrix,
    mixing_logit_matrix,
    mixing_final_matrix,
    feedforward_gate_expand,
    feedforward_shrink_matrix,
):
    seqs, cols, feats = homolog_matrix.shape
    rows, _, pair_width = contact_matrix.shape
    ch = tensor_product_matrices.shape[2] // 2
    heads = mixing_logit_matrix.shape[2]
    hidden = mixing_final_matrix.shape[1]
    head_width = hidden // heads
    ratio = R // C
    chunks = rows // 8
    pack = LANES // head_width
    groups = seqs // pack
    r = lax.axis_index("row")
    c = lax.axis_index("col")
    seq_ids = r * seqs + jnp.arange(seqs, dtype=jnp.int32)
    res_ids = c * cols + jnp.arange(cols, dtype=jnp.int32)
    seq_float = (seq_ids < genuine_homolog_total[0]).astype(F32)
    res_float = (res_ids < genuine_chain_length[0]).astype(F32)
    flipped = homolog_matrix.transpose(0, 2, 1)
    normed = standardize_features(homolog_matrix).astype(BF16)
    normed_flat = normed.transpose(1, 0, 2).reshape(cols, seqs * feats)
    left_w = tensor_product_matrices[0][:, :ch]
    right_w = tensor_product_matrices[0][:, ch:]
    right = jnp.einsum("sjf,fd->sdj", normed, right_w, preferred_element_type=F32)
    right = (right * (seq_float[:, None, None] * res_float[None, None, :])).astype(BF16)
    right = right.reshape(seqs, ch * cols)
    left = jnp.einsum("sjf,fc->sjc", normed, left_w, preferred_element_type=F32)
    left = (left * (seq_float[:, None, None] * res_float[None, :, None])).astype(BF16)
    left = left.reshape(seqs, ratio, rows * ch).transpose(1, 0, 2)
    outer_w = tensor_product_final[0].reshape(ch, ch, pair_width).transpose(2, 1, 0)
    outer_w = outer_w.reshape(pair_width, ch * ch)
    dims = (R, C, ratio, rows, cols, seqs * feats, heads, chunks)
    vmem = pl.BlockSpec(memory_space=pltpu.VMEM)
    smem = pl.BlockSpec(memory_space=pltpu.SMEM)
    dma = pltpu.SemaphoreType.DMA
    msa, pair_out = pl.pallas_call(
        functools.partial(kernel, dims),
        out_shape=(
            jax.ShapeDtypeStruct(flipped.shape, BF16),
            jax.ShapeDtypeStruct(contact_matrix.shape, BF16),
        ),
        in_specs=[smem] * 2 + [vmem] * 11,
        out_specs=(vmem, vmem),
        scratch_shapes=[
            pltpu.VMEM((R, seqs, ch * cols), BF16),
            pltpu.VMEM((R, seqs, rows * ch), BF16),
            pltpu.VMEM((C, cols, seqs * feats), BF16),
            pltpu.VMEM((chunks, 8, heads * cols), BF16),
            pltpu.VMEM((ratio, C, chunks, 8, heads * cols), BF16),
            pltpu.VMEM((2, heads, LANES), F32),
            pltpu.VMEM((ratio, C, 2, heads, LANES), F32),
            pltpu.VMEM((heads, 8, LANES), F32),
            pltpu.VMEM((R * seqs, ch * LANES), BF16),
            pltpu.VMEM((rows * ch, R * seqs), BF16),
            pltpu.VMEM((8, ch * ch, LANES), BF16),
            pltpu.VMEM((rows, cols, pair_width), BF16),
            pltpu.VMEM((rows, cols, pair_width), BF16),
            pltpu.VMEM((C * LANES, heads * groups * LANES), BF16),
            pltpu.VMEM((cols, heads * groups * LANES), F32),
            pltpu.VMEM((cols, heads * groups * LANES), BF16),
            pltpu.VMEM((pack * feats, heads * LANES), BF16),
            pltpu.VMEM((pack * feats, heads * LANES), BF16),
            pltpu.VMEM((pack * feats, heads * LANES), BF16),
            dma((R,)), dma((R,)), dma((ratio, C)), dma((R,)), dma((C,)), dma((C,)),
            dma((chunks, R)), dma((ratio, C, chunks)), dma((R,)), dma((ratio, C)),
        ],
        compiler_params=pltpu.CompilerParams(
            collective_id=0, has_side_effects=True, vmem_limit_bytes=60 * 1024 * 1024
        ),
        name="msa_block",
    )(
        genuine_homolog_total, genuine_chain_length,
        right, left, normed_flat, flipped, contact_matrix,
        outer_w, mixing_value_gate_matrix[0], mixing_logit_matrix[0].T, mixing_final_matrix[0].T,
        feedforward_gate_expand[0], feedforward_shrink_matrix[0],
    )
    return (msa.transpose(0, 2, 1), pair_out)


def solution(mesh):
    in_specs = (P("row", "col", None), P("row", "col", None)) + (P(),) * 9
    out_specs = (P("row", "col", None), P("row", "col", None))
    body = functools.partial(local, mesh.shape["row"], mesh.shape["col"])
    return jax.shard_map(body, mesh=mesh, in_specs=in_specs, out_specs=out_specs, check_vma=False)
```

```python
import functools

import jax
import jax.numpy as jnp
from jax import lax
from jax.experimental import pallas as pl
from jax.experimental.pallas import tpu as pltpu
from jax.sharding import PartitionSpec as P

EPSILON = 1e-05
MASKED = -1000000000.0
MESH = pl.DeviceIdType.MESH
LANES = 128
BF16 = jnp.bfloat16
F32 = jnp.float32


def standardize_features(field):
    field = field.astype(F32)
    center = field - jnp.mean(field, axis=-1, keepdims=True)
    spread = jnp.mean(center * center, axis=-1, keepdims=True)
    return center * lax.rsqrt(spread + EPSILON)


def flip(index, mask):
    bit = 1
    while bit <= mask:
        if mask & bit:
            index = index + bit - 2 * bit * ((index // bit) % 2)
        bit *= 2
    return index


def kernel(
    dims,
    seqs_ref, length_ref,
    homolog_ref, pair_ref, project_ref,
    outer_ref, mix_ref, logit_w_ref, mix_out_ref, up_ref, down_ref,
    msa_ref, out_ref,
    right_buf, left_buf, normed_buf, logit_send, logit_buf, stat_send, stat_buf, expo_tile,
    right_all, left_all, product, pair_new, pair_normed, values, gates, gated,
    value_w_ref, gate_w_ref, final_w_ref, right_ref, left_ref, normed_ref, tile_a, tile_b, outer_w_ref, outer_f32,
    s_right, r_right, s_left, r_left, s_norm, r_norm, s_logit, r_logit, s_stat, r_stat,
):
    R, C, ratio, rows, cols, width, heads, chunks = dims
    r = lax.axis_index("row")
    c = lax.axis_index("col")
    home = r // ratio

    barrier = pltpu.get_barrier_semaphore()

    def greet(row, col):
        pl.semaphore_signal(barrier, inc=1, device_id=(row, col), device_id_type=MESH)

    for t in range(1, R):
        greet((r + t) % R, c)
    for t in range(1, C):
        greet(r, (c + t) % C)
    for t in range(R):
        row = (r + t) % R

        @pl.when(jnp.logical_not((row == r) & (home == c)))
        def _():
            greet(row, home)

    for h in range(ratio):
        for t in range(C):
            row, col = c * ratio + h, (c + t) % C

            @pl.when(jnp.logical_not((row == r) & (col == c)))
            def _():
                greet(row, col)

    seqs, feats, _ = homolog_ref.shape
    half_width = project_ref.shape[1] // 2
    field = homolog_ref[...].astype(F32)
    center = field - jnp.mean(field, axis=1, keepdims=True)
    spread = jnp.mean(center * center, axis=1, keepdims=True)
    normed_t = center * lax.rsqrt(spread + EPSILON)
    normed_ref[...] = normed_t.reshape(width, cols).T.astype(BF16)
    project_t = project_ref[...].astype(F32).T.astype(BF16)
    along = c * cols + lax.broadcasted_iota(jnp.int32, (half_width, cols), 1) < length_ref[0]
    down = c * cols + lax.broadcasted_iota(jnp.int32, (cols, half_width), 0) < length_ref[0]
    for n in range(seqs):
        there = r * seqs + n < seqs_ref[0]
        side = jnp.dot(
            project_t[half_width:], normed_t[n].astype(BF16), preferred_element_type=F32)
        tile_a[n * half_width:(n + 1) * half_width, 0:cols] = jnp.where(along & there, side, 0.0)
        side = jnp.dot(
            normed_ref[:, n * feats:(n + 1) * feats], project_ref[:, :half_width],
            preferred_element_type=F32)
        tile_b[n * cols:(n + 1) * cols, 0:half_width] = jnp.where(down & there, side, 0.0)
    right_ref[...] = jnp.concatenate(
        [tile_a[pl.ds(d, seqs, stride=half_width), :][:, :cols] for d in range(half_width)],
        axis=1).astype(BF16)
    for h in range(ratio):
        left_ref[h] = jnp.concatenate(
            [tile_b[pl.ds(h * rows + i, seqs, stride=cols), :][:, :half_width]
             for i in range(rows)], axis=1).astype(BF16)

    own = jnp.where(home == c, 1, 0)
    pl.semaphore_wait(barrier, (R - 1) + (C - 1) + 2 * R - 2 * own)

    def right_copy(n):
        root = flip(r, n & (n - 1))
        return pltpu.make_async_remote_copy(
            src_ref=right_buf.at[root] if n & (n - 1) else right_ref,
            dst_ref=right_buf.at[root],
            send_sem=s_right.at[n], recv_sem=r_right.at[n],
            device_id=(flip(r, n & -n), c), device_id_type=MESH)

    def left_copy(h, t):
        return pltpu.make_async_remote_copy(
            src_ref=left_ref.at[h], dst_ref=left_buf.at[r],
            send_sem=s_left.at[h, t], recv_sem=r_left.at[r],
            device_id=(c * ratio + h, (c + t) % C), device_id_type=MESH)

    def norm_copy(t):
        return pltpu.make_async_remote_copy(
            src_ref=normed_ref, dst_ref=normed_buf.at[c],
            send_sem=s_norm.at[t], recv_sem=r_norm.at[c],
            device_id=(r, (c + t) % C), device_id_type=MESH)

    def logit_copy(k, t):
        return pltpu.make_async_remote_copy(
            src_ref=logit_send.at[k], dst_ref=logit_buf.at[r % ratio, c, k],
            send_sem=s_logit.at[k, t], recv_sem=r_logit.at[r % ratio, c, k],
            device_id=((r + t) % R, home), device_id_type=MESH)

    def stat_copy(t):
        return pltpu.make_async_remote_copy(
            src_ref=stat_send, dst_ref=stat_buf.at[r % ratio, c],
            send_sem=s_stat.at[t], recv_sem=r_stat.at[r % ratio, c],
            device_id=((r + t) % R, home), device_id_type=MESH)

    for h in range(ratio):
        for t in range(C):
            mine = (c * ratio + h == r) & (t == 0)

            @pl.when(jnp.logical_not(mine))
            def _():
                left_copy(h, t).start()

            @pl.when(mine)
            def _():
                left_buf[r] = left_ref[h]

    steps = [R >> (e + 1) for e in range(R.bit_length() - 1)]
    for bit in steps:
        right_copy(bit).start()
    right_buf[r] = right_ref[...]
    normed_buf[c] = normed_ref[...]

    def wait_left(src):
        pltpu.make_async_remote_copy(
            src_ref=left_ref.at[0], dst_ref=left_buf.at[src],
            send_sem=s_left.at[0, 0], recv_sem=r_left.at[src],
            device_id=(src, home), device_id_type=MESH).wait_recv()

    def wait_right(n):
        pltpu.make_async_remote_copy(
            src_ref=right_ref, dst_ref=right_buf.at[flip(r, n)],
            send_sem=s_right.at[n], recv_sem=r_right.at[n],
            device_id=(flip(r, n & -n), c), device_id_type=MESH).wait_recv()

    def wait_norm(src):
        pltpu.make_async_remote_copy(
            src_ref=normed_ref, dst_ref=normed_buf.at[src],
            send_sem=s_norm.at[0], recv_sem=r_norm.at[src],
            device_id=(r, src), device_id_type=MESH).wait_recv()

    outer_f32[...] = outer_ref[...].astype(F32)
    quad = LANES // half_width
    for d in range(0, half_width, quad):
        outer_w_ref[:, d * half_width:(d + quad) * half_width] = jnp.concatenate(
            [outer_f32[pl.ds(d + e, half_width, stride=half_width), :] for e in range(quad)],
            axis=0).T.astype(BF16)

    hidden_width = mix_out_ref.shape[1]
    head_width = hidden_width // heads
    pack = LANES // head_width
    shape = (pack * feats, feats)
    stack = (lax.broadcasted_iota(jnp.int32, shape, 0) % feats
             == lax.broadcasted_iota(jnp.int32, shape, 1)).astype(F32).astype(BF16)
    shape = (hidden_width, heads * LANES)
    row, lane = (lax.broadcasted_iota(jnp.int32, shape, axis) for axis in (0, 1))
    widen = ((row // head_width == lane // LANES) & (row % head_width == lane % head_width))
    widen = widen.astype(F32).astype(BF16)
    shape = (pack * feats, heads * LANES)
    row, lane = (lax.broadcasted_iota(jnp.int32, shape, axis) for axis in (0, 1))
    diagonal = row // feats == lane % LANES // head_width
    for source, target in (
        (mix_ref[:, :hidden_width], value_w_ref),
        (mix_ref[:, hidden_width:], gate_w_ref),
        (mix_out_ref[...], final_w_ref),
    ):
        tall = jnp.dot(stack, source, preferred_element_type=F32).astype(BF16)
        wide = jnp.dot(tall, widen, preferred_element_type=F32)
        target[...] = jnp.where(diagonal, wide, 0.0).astype(BF16)

    for n in sorted(range(1, R), key=lambda n: (bin(n).count("1"), -(n & -n))):
        wait_right(n)
        for bit in steps:
            if bit < n & -n:
                right_copy(n + bit).start()

    for t in range(1, C):
        norm_copy(t).start()

    groups = gates.shape[1] // (heads * LANES)
    group_width = width // groups
    for g in range(groups):
        part = jnp.dot(
            normed_ref[:, g * group_width:(g + 1) * group_width], gate_w_ref[...],
            preferred_element_type=F32)
        for h in range(heads):
            at = (h * groups + g) * LANES
            gates[:, at:at + LANES] = jax.nn.sigmoid(part[:, h * LANES:(h + 1) * LANES])
    values[...] = jnp.zeros_like(values)
    stat_send[...] = jnp.zeros_like(stat_send)

    for src in range(R):
        @pl.when(jnp.logical_not((src == r) & (home == c)))
        def _():
            wait_left(src)

    left_t = left_buf[...].astype(F32).reshape(R * left_buf.shape[1], left_buf.shape[2]).T
    left_all[...] = left_t.astype(BF16)
    right_flat = right_buf[...].astype(F32).reshape(right_all.shape[0], right_buf.shape[2])
    zeros = jnp.zeros((right_all.shape[0], LANES - cols), F32)
    for d in range(right_buf.shape[2] // cols):
        right_all[:, d * LANES:(d + 1) * LANES] = jnp.concatenate(
            [right_flat[:, d * cols:(d + 1) * cols], zeros], axis=1).astype(BF16)

    inverse = 1.0 / jnp.maximum(seqs_ref[0].astype(F32), 1.0)
    ch = product.shape[1] // (right_all.shape[1] // LANES)

    def send_logits(k):
        for t in range(R):
            if t > 0:
                logit_copy(k, t).start()
            else:
                @pl.when(home == c)
                def _():
                    logit_buf[r % ratio, c, k] = logit_send[k]

                @pl.when(home != c)
                def _():
                    logit_copy(k, 0).start()

    row_lane = lax.broadcasted_iota(jnp.int32, (heads, LANES), 1)
    real = c * cols + lax.broadcasted_iota(jnp.int32, (heads, cols), 1) < length_ref[0]

    def outer_step(k, carry):
        @pl.when(k > 0)
        def _():
            send_logits(k - 1)

        lhs = left_all[pl.ds(pl.multiple_of(k * 8 * ch, 8 * ch), 8 * ch), :]
        for d in range(0, right_all.shape[1] // LANES, 2):
            p = jnp.dot(lhs, right_all[:, d * LANES:(d + 2) * LANES], preferred_element_type=F32)
            p = (p * inverse).astype(BF16)
            for e in range(2):
                product[:, (d + e) * ch:(d + e + 1) * ch, :] = p[
                    :, e * LANES:(e + 1) * LANES].reshape(8, ch, LANES)
        for q in range(0, 8, 2):
            both = jnp.concatenate([product[q], product[q + 1]], axis=1)
            update = jnp.dot(outer_w_ref[...], both, preferred_element_type=F32)
            for e in range(2):
                i = k * 8 + q + e
                step = update[:, e * LANES:(e + 1) * LANES].T[:cols]
                pair = (pair_ref[i].astype(F32) + step).astype(BF16)
                pair_new[i] = pair
                normed = standardize_features(pair).astype(BF16)
                pair_normed[i] = normed
                logits = lax.dot_general(
                    logit_w_ref[...], normed, (((1,), (1,)), ((), ())),
                    preferred_element_type=F32)
                logits = jnp.where(real, logits, MASKED)
                peak = jnp.max(logits, axis=1, keepdims=True)
                expo = jnp.exp(logits - peak)
                expo_tile[:, q + e, 0:cols] = expo
                stat_send[0] = jnp.where(row_lane == i, peak, stat_send[0])
                stat_send[1] = jnp.where(
                    row_lane == i, jnp.sum(expo, axis=1, keepdims=True), stat_send[1])
        logit_send[k] = jnp.concatenate(
            [expo_tile[h, :, 0:cols] for h in range(heads)], axis=1).astype(BF16)
        return carry

    lax.fori_loop(0, chunks, outer_step, 0)
    send_logits(chunks - 1)
    for t in range(R):
        if t > 0:
            stat_copy(t).start()
        else:
            @pl.when(home == c)
            def _():
                stat_buf[r % ratio, c] = stat_send[...]

            @pl.when(home != c)
            def _():
                stat_copy(0).start()

    trans = down_ref.shape[0]

    def transition_step(k, carry):
        normed = pair_normed[pl.ds(k * 4, 4)].reshape(4 * cols, LANES)
        hidden = jnp.dot(normed, up_ref[...], preferred_element_type=F32)
        front, back = hidden[:, :trans], hidden[:, trans:]
        active = (front / (1.0 + jnp.exp(-front)) * back).astype(BF16)
        update = jnp.dot(active, down_ref[...], preferred_element_type=F32)
        pair = pair_new[pl.ds(k * 4, 4)].astype(F32) + update.reshape(4, cols, LANES)
        out_ref[pl.ds(k * 4, 4)] = pair.astype(BF16)
        return carry

    lax.fori_loop(0, rows // 4, transition_step, 0)

    for t in range(1, C):
        wait_norm((c + t) % C)
    for src in range(C):
        for g in range(groups):
            part = jnp.dot(
                normed_buf[src, :, g * group_width:(g + 1) * group_width], value_w_ref[...],
                preferred_element_type=F32).astype(BF16)
            for h in range(heads):
                at = (h * groups + g) * LANES
                values[src * LANES:src * LANES + cols, at:at + LANES] = part[
                    :, h * LANES:(h + 1) * LANES]

    for h in range(ratio):
        for src in range(C):
            @pl.when(jnp.logical_not((c * ratio + h == r) & (src == c)))
            def _():
                for k in range(chunks):
                    pltpu.make_async_remote_copy(
                        src_ref=logit_send.at[k], dst_ref=logit_buf.at[h, src, k],
                        send_sem=s_logit.at[k, 0], recv_sem=r_logit.at[h, src, k],
                        device_id=(r, home), device_id_type=MESH).wait_recv()
                pltpu.make_async_remote_copy(
                    src_ref=stat_send, dst_ref=stat_buf.at[h, src],
                    send_sem=s_stat.at[0], recv_sem=r_stat.at[h, src],
                    device_id=(r, home), device_id_type=MESH).wait_recv()

    scales = []
    for half in range(ratio):
        peaks = [stat_buf[half, src, 0] for src in range(C)]
        top = functools.reduce(jnp.maximum, peaks)
        shifts = [jnp.exp(peak - top) for peak in peaks]
        total = sum(shift * stat_buf[half, src, 1] for src, shift in enumerate(shifts))
        total = jnp.where(row_lane < rows, total, 1.0)
        scales.append([(shift / total).T for shift in shifts])
    gap = jnp.zeros((rows, LANES - cols), F32)
    expos = [[logit_buf[half, src].astype(F32).reshape(rows, heads * cols) for src in range(C)]
             for half in range(ratio)]
    span = groups * LANES
    for h in range(heads):
        weights = jnp.concatenate([
            jnp.concatenate([
                piece for src in range(C) for piece in (
                    expos[half][src][:, h * cols:(h + 1) * cols]
                    * scales[half][src][:rows, h:h + 1], gap)], axis=1)
            for half in range(ratio)], axis=0).astype(BF16)
        mean = jnp.dot(weights, values[:, h * span:(h + 1) * span], preferred_element_type=F32)
        mixed = (gates[:, h * span:(h + 1) * span] * mean).astype(BF16)
        for g in range(groups):
            at = (g * heads + h) * LANES
            gated[:, at:at + LANES] = mixed[:, g * LANES:(g + 1) * LANES]
    for g in range(groups):
        part = lax.dot_general(
            gated[:, g * heads * LANES:(g + 1) * heads * LANES], final_w_ref[...],
            (((1,), (1,)), ((), ())), preferred_element_type=F32)
        sl = slice(g * pack, (g + 1) * pack)
        msa_ref[sl] = (
            homolog_ref[sl].astype(F32) + part.T.reshape(pack, feats, cols)).astype(BF16)

    for t in range(1, R):
        right_copy(t).wait_send()
    for t in range(1, C):
        norm_copy(t).wait_send()
    for h in range(ratio):
        for t in range(C):
            @pl.when(jnp.logical_not((c * ratio + h == r) & (t == 0)))
            def _():
                left_copy(h, t).wait_send()

    def finish(k, carry):
        for t in range(1, R):
            logit_copy(k, t).wait_send()

        @pl.when(home != c)
        def _():
            logit_copy(k, 0).wait_send()

        return carry

    for t in range(1, R):
        stat_copy(t).wait_send()

    @pl.when(home != c)
    def _():
        stat_copy(0).wait_send()

    lax.fori_loop(0, chunks, finish, 0)


def local(
    R,
    C,
    homolog_matrix,
    contact_matrix,
    genuine_homolog_total,
    genuine_chain_length,
    tensor_product_matrices,
    tensor_product_final,
    mixing_value_gate_matrix,
    mixing_logit_matrix,
    mixing_final_matrix,
    feedforward_gate_expand,
    feedforward_shrink_matrix,
):
    seqs, cols, feats = homolog_matrix.shape
    rows, _, pair_width = contact_matrix.shape
    ch = tensor_product_matrices.shape[2] // 2
    heads = mixing_logit_matrix.shape[2]
    hidden = mixing_final_matrix.shape[1]
    head_width = hidden // heads
    ratio = R // C
    chunks = rows // 8
    pack = LANES // head_width
    groups = seqs // pack
    flipped = homolog_matrix.transpose(0, 2, 1)
    dims = (R, C, ratio, rows, cols, seqs * feats, heads, chunks)
    vmem = pl.BlockSpec(memory_space=pltpu.VMEM)
    smem = pl.BlockSpec(memory_space=pltpu.SMEM)
    dma = pltpu.SemaphoreType.DMA
    msa, pair_out = pl.pallas_call(
        functools.partial(kernel, dims),
        out_shape=(
            jax.ShapeDtypeStruct(flipped.shape, BF16),
            jax.ShapeDtypeStruct(contact_matrix.shape, BF16),
        ),
        in_specs=[smem] * 2 + [vmem] * 9,
        out_specs=(vmem, vmem),
        scratch_shapes=[
            pltpu.VMEM((R, seqs, ch * cols), BF16),
            pltpu.VMEM((R, seqs, rows * ch), BF16),
            pltpu.VMEM((C, cols, seqs * feats), BF16),
            pltpu.VMEM((chunks, 8, heads * cols), BF16),
            pltpu.VMEM((ratio, C, chunks, 8, heads * cols), BF16),
            pltpu.VMEM((2, heads, LANES), F32),
            pltpu.VMEM((ratio, C, 2, heads, LANES), F32),
            pltpu.VMEM((heads, 8, LANES), F32),
            pltpu.VMEM((R * seqs, ch * LANES), BF16),
            pltpu.VMEM((rows * ch, R * seqs), BF16),
            pltpu.VMEM((8, ch * ch, LANES), BF16),
            pltpu.VMEM((rows, cols, pair_width), BF16),
            pltpu.VMEM((rows, cols, pair_width), BF16),
            pltpu.VMEM((C * LANES, heads * groups * LANES), BF16),
            pltpu.VMEM((cols, heads * groups * LANES), F32),
            pltpu.VMEM((cols, heads * groups * LANES), BF16),
            pltpu.VMEM((pack * feats, heads * LANES), BF16),
            pltpu.VMEM((pack * feats, heads * LANES), BF16),
            pltpu.VMEM((pack * feats, heads * LANES), BF16),
            pltpu.VMEM((seqs, ch * cols), BF16),
            pltpu.VMEM((ratio, seqs, rows * ch), BF16),
            pltpu.VMEM((cols, seqs * feats), BF16),
            pltpu.VMEM((seqs * ch, LANES), F32),
            pltpu.VMEM((seqs * cols, LANES), F32),
            pltpu.VMEM((pair_width, ch * ch), BF16),
            pltpu.VMEM((ch * ch, pair_width), F32),
            dma((R,)), dma((R,)), dma((ratio, C)), dma((R,)), dma((C,)), dma((C,)),
            dma((chunks, R)), dma((ratio, C, chunks)), dma((R,)), dma((ratio, C)),
        ],
        compiler_params=pltpu.CompilerParams(
            collective_id=0, has_side_effects=True, vmem_limit_bytes=60 * 1024 * 1024
        ),
        name="msa_block",
    )(
        genuine_homolog_total, genuine_chain_length,
        flipped, contact_matrix, tensor_product_matrices[0],
        tensor_product_final[0], mixing_value_gate_matrix[0], mixing_logit_matrix[0].T, mixing_final_matrix[0].T,
        feedforward_gate_expand[0], feedforward_shrink_matrix[0],
    )
    return (msa.transpose(0, 2, 1), pair_out)


def solution(mesh):
    in_specs = (P("row", "col", None), P("row", "col", None)) + (P(),) * 9
    out_specs = (P("row", "col", None), P("row", "col", None))
    body = functools.partial(local, mesh.shape["row"], mesh.shape["col"])
    return jax.shard_map(body, mesh=mesh, in_specs=in_specs, out_specs=out_specs, check_vma=False)
```

```python
import functools

import jax
import jax.numpy as jnp
from jax import lax
from jax.experimental import pallas as pl
from jax.experimental.pallas import tpu as pltpu
from jax.sharding import PartitionSpec as P

EPSILON = 1e-05
MASKED = -1000000000.0
MESH = pl.DeviceIdType.MESH
LANES = 128
BF16 = jnp.bfloat16
F32 = jnp.float32


def standardize_features(field):
    field = field.astype(F32)
    center = field - jnp.mean(field, axis=-1, keepdims=True)
    spread = jnp.mean(center * center, axis=-1, keepdims=True)
    return center * lax.rsqrt(spread + EPSILON)


def flip(index, mask):
    bit = 1
    while bit <= mask:
        if mask & bit:
            index = index + bit - 2 * bit * ((index // bit) % 2)
        bit *= 2
    return index


def kernel(
    dims,
    seqs_ref, length_ref,
    homolog_ref, pair_ref, project_ref,
    outer_ref, mix_ref, logit_w_ref, mix_out_ref, up_ref, down_ref,
    msa_ref, out_ref,
    right_buf, left_buf, normed_buf, logit_send, logit_buf, stat_send, stat_buf, expo_tile,
    right_all, left_all, product, pair_new, pair_normed, values, gates, gated,
    value_w_ref, gate_w_ref, final_w_ref, right_ref, left_ref, normed_ref, tile_a, tile_b, outer_w_ref, outer_f32,
    s_right, r_right, s_left, r_left, s_norm, r_norm, s_logit, r_logit, s_stat, r_stat,
):
    R, C, ratio, rows, cols, width, heads, chunks = dims
    r = lax.axis_index("row")
    c = lax.axis_index("col")
    home = r // ratio

    barrier = pltpu.get_barrier_semaphore()

    def greet(row, col):
        pl.semaphore_signal(barrier, inc=1, device_id=(row, col), device_id_type=MESH)

    for t in range(1, R):
        greet((r + t) % R, c)
    for t in range(1, C):
        greet(r, (c + t) % C)
    for t in range(R):
        row = (r + t) % R

        @pl.when(jnp.logical_not((row == r) & (home == c)))
        def _():
            greet(row, home)

    for h in range(ratio):
        for t in range(C):
            row, col = c * ratio + h, (c + t) % C

            @pl.when(jnp.logical_not((row == r) & (col == c)))
            def _():
                greet(row, col)

    seqs, feats, _ = homolog_ref.shape
    half_width = project_ref.shape[1] // 2
    field = homolog_ref[...].astype(F32)
    center = field - jnp.mean(field, axis=1, keepdims=True)
    spread = jnp.mean(center * center, axis=1, keepdims=True)
    normed_t = center * lax.rsqrt(spread + EPSILON)
    normed_ref[...] = normed_t.reshape(width, cols).T.astype(BF16)
    project_t = project_ref[...].astype(F32).T.astype(BF16)
    along = c * cols + lax.broadcasted_iota(jnp.int32, (half_width, cols), 1) < length_ref[0]
    down = c * cols + lax.broadcasted_iota(jnp.int32, (cols, half_width), 0) < length_ref[0]
    for n in range(seqs):
        there = r * seqs + n < seqs_ref[0]
        side = jnp.dot(
            project_t[half_width:], normed_t[n].astype(BF16), preferred_element_type=F32)
        tile_a[n * half_width:(n + 1) * half_width, 0:cols] = jnp.where(along & there, side, 0.0)
        side = jnp.dot(
            normed_ref[:, n * feats:(n + 1) * feats], project_ref[:, :half_width],
            preferred_element_type=F32)
        tile_b[n * cols:(n + 1) * cols, 0:half_width] = jnp.where(down & there, side, 0.0)
    right_ref[...] = jnp.concatenate(
        [tile_a[pl.ds(d, seqs, stride=half_width), :][:, :cols] for d in range(half_width)],
        axis=1).astype(BF16)
    for h in range(ratio):
        left_ref[h] = jnp.concatenate(
            [tile_b[pl.ds(h * rows + i, seqs, stride=cols), :][:, :half_width]
             for i in range(rows)], axis=1).astype(BF16)

    own = jnp.where(home == c, 1, 0)
    pl.semaphore_wait(barrier, (R - 1) + (C - 1) + 2 * R - 2 * own)

    def right_copy(n):
        root = flip(r, n & (n - 1))
        return pltpu.make_async_remote_copy(
            src_ref=right_buf.at[root] if n & (n - 1) else right_ref,
            dst_ref=right_buf.at[root],
            send_sem=s_right.at[n], recv_sem=r_right.at[n],
            device_id=(flip(r, n & -n), c), device_id_type=MESH)

    def left_copy(h, t):
        return pltpu.make_async_remote_copy(
            src_ref=left_ref.at[h], dst_ref=left_buf.at[r],
            send_sem=s_left.at[h, t], recv_sem=r_left.at[r],
            device_id=(c * ratio + h, (c + t) % C), device_id_type=MESH)

    def norm_copy(t):
        return pltpu.make_async_remote_copy(
            src_ref=normed_ref, dst_ref=normed_buf.at[c],
            send_sem=s_norm.at[t], recv_sem=r_norm.at[c],
            device_id=(r, (c + t) % C), device_id_type=MESH)

    def logit_copy(k, t):
        return pltpu.make_async_remote_copy(
            src_ref=logit_send.at[k], dst_ref=logit_buf.at[r % ratio, c, k],
            send_sem=s_logit.at[k, t], recv_sem=r_logit.at[r % ratio, c, k],
            device_id=((r + t) % R, home), device_id_type=MESH)

    def stat_copy(t):
        return pltpu.make_async_remote_copy(
            src_ref=stat_send, dst_ref=stat_buf.at[r % ratio, c],
            send_sem=s_stat.at[t], recv_sem=r_stat.at[r % ratio, c],
            device_id=((r + t) % R, home), device_id_type=MESH)

    steps = [R >> (e + 1) for e in range(R.bit_length() - 1)]
    for bit in steps:
        right_copy(bit).start()
    for h in range(ratio):
        for t in range(C):
            mine = (c * ratio + h == r) & (t == 0)

            @pl.when(jnp.logical_not(mine))
            def _():
                left_copy(h, t).start()

            @pl.when(mine)
            def _():
                left_buf[r] = left_ref[h]

    right_buf[r] = right_ref[...]
    normed_buf[c] = normed_ref[...]

    def wait_left(src):
        pltpu.make_async_remote_copy(
            src_ref=left_ref.at[0], dst_ref=left_buf.at[src],
            send_sem=s_left.at[0, 0], recv_sem=r_left.at[src],
            device_id=(src, home), device_id_type=MESH).wait_recv()

    def wait_right(n):
        pltpu.make_async_remote_copy(
            src_ref=right_ref, dst_ref=right_buf.at[flip(r, n)],
            send_sem=s_right.at[n], recv_sem=r_right.at[n],
            device_id=(flip(r, n & -n), c), device_id_type=MESH).wait_recv()

    def wait_norm(src):
        pltpu.make_async_remote_copy(
            src_ref=normed_ref, dst_ref=normed_buf.at[src],
            send_sem=s_norm.at[0], recv_sem=r_norm.at[src],
            device_id=(r, src), device_id_type=MESH).wait_recv()

    outer_f32[...] = outer_ref[...].astype(F32)
    quad = LANES // half_width
    for d in range(0, half_width, quad):
        outer_w_ref[:, d * half_width:(d + quad) * half_width] = jnp.concatenate(
            [outer_f32[pl.ds(d + e, half_width, stride=half_width), :] for e in range(quad)],
            axis=0).T.astype(BF16)

    hidden_width = mix_out_ref.shape[1]
    head_width = hidden_width // heads
    pack = LANES // head_width
    shape = (pack * feats, feats)
    stack = (lax.broadcasted_iota(jnp.int32, shape, 0) % feats
             == lax.broadcasted_iota(jnp.int32, shape, 1)).astype(F32).astype(BF16)
    shape = (hidden_width, heads * LANES)
    row, lane = (lax.broadcasted_iota(jnp.int32, shape, axis) for axis in (0, 1))
    widen = ((row // head_width == lane // LANES) & (row % head_width == lane % head_width))
    widen = widen.astype(F32).astype(BF16)
    shape = (pack * feats, heads * LANES)
    row, lane = (lax.broadcasted_iota(jnp.int32, shape, axis) for axis in (0, 1))
    diagonal = row // feats == lane % LANES // head_width
    for source, target in (
        (mix_ref[:, :hidden_width], value_w_ref),
        (mix_ref[:, hidden_width:], gate_w_ref),
        (mix_out_ref[...], final_w_ref),
    ):
        tall = jnp.dot(stack, source, preferred_element_type=F32).astype(BF16)
        wide = jnp.dot(tall, widen, preferred_element_type=F32)
        target[...] = jnp.where(diagonal, wide, 0.0).astype(BF16)

    for n in sorted(range(1, R), key=lambda n: (bin(n).count("1"), -(n & -n))):
        wait_right(n)
        for bit in steps:
            if bit < n & -n:
                right_copy(n + bit).start()

    for t in range(1, C):
        norm_copy(t).start()

    groups = gates.shape[1] // (heads * LANES)
    group_width = width // groups
    for g in range(groups):
        part = jnp.dot(
            normed_ref[:, g * group_width:(g + 1) * group_width], gate_w_ref[...],
            preferred_element_type=F32)
        for h in range(heads):
            at = (h * groups + g) * LANES
            gates[:, at:at + LANES] = jax.nn.sigmoid(part[:, h * LANES:(h + 1) * LANES])
    values[...] = jnp.zeros_like(values)
    stat_send[...] = jnp.zeros_like(stat_send)

    for src in range(R):
        @pl.when(jnp.logical_not((src == r) & (home == c)))
        def _():
            wait_left(src)

    left_t = left_buf[...].astype(F32).reshape(R * left_buf.shape[1], left_buf.shape[2]).T
    left_all[...] = left_t.astype(BF16)
    right_flat = right_buf[...].astype(F32).reshape(right_all.shape[0], right_buf.shape[2])
    zeros = jnp.zeros((right_all.shape[0], LANES - cols), F32)
    for d in range(right_buf.shape[2] // cols):
        right_all[:, d * LANES:(d + 1) * LANES] = jnp.concatenate(
            [right_flat[:, d * cols:(d + 1) * cols], zeros], axis=1).astype(BF16)

    inverse = 1.0 / jnp.maximum(seqs_ref[0].astype(F32), 1.0)
    ch = product.shape[1] // (right_all.shape[1] // LANES)

    def send_logits(k):
        for t in range(R):
            if t > 0:
                logit_copy(k, t).start()
            else:
                @pl.when(home == c)
                def _():
                    logit_buf[r % ratio, c, k] = logit_send[k]

                @pl.when(home != c)
                def _():
                    logit_copy(k, 0).start()

    row_lane = lax.broadcasted_iota(jnp.int32, (heads, LANES), 1)
    real = c * cols + lax.broadcasted_iota(jnp.int32, (heads, cols), 1) < length_ref[0]

    def outer_step(k, carry):
        @pl.when(k > 0)
        def _():
            send_logits(k - 1)

        lhs = left_all[pl.ds(pl.multiple_of(k * 8 * ch, 8 * ch), 8 * ch), :]
        for d in range(0, right_all.shape[1] // LANES, 2):
            p = jnp.dot(lhs, right_all[:, d * LANES:(d + 2) * LANES], preferred_element_type=F32)
            p = (p * inverse).astype(BF16)
            for e in range(2):
                product[:, (d + e) * ch:(d + e + 1) * ch, :] = p[
                    :, e * LANES:(e + 1) * LANES].reshape(8, ch, LANES)
        for q in range(0, 8, 2):
            both = jnp.concatenate([product[q], product[q + 1]], axis=1)
            update = jnp.dot(outer_w_ref[...], both, preferred_element_type=F32)
            for e in range(2):
                i = k * 8 + q + e
                step = update[:, e * LANES:(e + 1) * LANES].T[:cols]
                pair = (pair_ref[i].astype(F32) + step).astype(BF16)
                pair_new[i] = pair
                normed = standardize_features(pair).astype(BF16)
                pair_normed[i] = normed
                logits = lax.dot_general(
                    logit_w_ref[...], normed, (((1,), (1,)), ((), ())),
                    preferred_element_type=F32)
                logits = jnp.where(real, logits, MASKED)
                peak = jnp.max(logits, axis=1, keepdims=True)
                expo = jnp.exp(logits - peak)
                expo_tile[:, q + e, 0:cols] = expo
                stat_send[0] = jnp.where(row_lane == i, peak, stat_send[0])
                stat_send[1] = jnp.where(
                    row_lane == i, jnp.sum(expo, axis=1, keepdims=True), stat_send[1])
        logit_send[k] = jnp.concatenate(
            [expo_tile[h, :, 0:cols] for h in range(heads)], axis=1).astype(BF16)
        return carry

    lax.fori_loop(0, chunks, outer_step, 0)
    send_logits(chunks - 1)
    for t in range(R):
        if t > 0:
            stat_copy(t).start()
        else:
            @pl.when(home == c)
            def _():
                stat_buf[r % ratio, c] = stat_send[...]

            @pl.when(home != c)
            def _():
                stat_copy(0).start()

    trans = down_ref.shape[0]

    def transition_step(k, carry):
        normed = pair_normed[pl.ds(k * 4, 4)].reshape(4 * cols, LANES)
        hidden = jnp.dot(normed, up_ref[...], preferred_element_type=F32)
        front, back = hidden[:, :trans], hidden[:, trans:]
        active = (front / (1.0 + jnp.exp(-front)) * back).astype(BF16)
        update = jnp.dot(active, down_ref[...], preferred_element_type=F32)
        pair = pair_new[pl.ds(k * 4, 4)].astype(F32) + update.reshape(4, cols, LANES)
        out_ref[pl.ds(k * 4, 4)] = pair.astype(BF16)
        return carry

    lax.fori_loop(0, rows // 4, transition_step, 0)

    for t in range(1, C):
        wait_norm((c + t) % C)
    for src in range(C):
        for g in range(groups):
            part = jnp.dot(
                normed_buf[src, :, g * group_width:(g + 1) * group_width], value_w_ref[...],
                preferred_element_type=F32).astype(BF16)
            for h in range(heads):
                at = (h * groups + g) * LANES
                values[src * LANES:src * LANES + cols, at:at + LANES] = part[
                    :, h * LANES:(h + 1) * LANES]

    for h in range(ratio):
        for src in range(C):
            @pl.when(jnp.logical_not((c * ratio + h == r) & (src == c)))
            def _():
                for k in range(chunks):
                    pltpu.make_async_remote_copy(
                        src_ref=logit_send.at[k], dst_ref=logit_buf.at[h, src, k],
                        send_sem=s_logit.at[k, 0], recv_sem=r_logit.at[h, src, k],
                        device_id=(r, home), device_id_type=MESH).wait_recv()
                pltpu.make_async_remote_copy(
                    src_ref=stat_send, dst_ref=stat_buf.at[h, src],
                    send_sem=s_stat.at[0], recv_sem=r_stat.at[h, src],
                    device_id=(r, home), device_id_type=MESH).wait_recv()

    scales = []
    for half in range(ratio):
        peaks = [stat_buf[half, src, 0] for src in range(C)]
        top = functools.reduce(jnp.maximum, peaks)
        shifts = [jnp.exp(peak - top) for peak in peaks]
        total = sum(shift * stat_buf[half, src, 1] for src, shift in enumerate(shifts))
        total = jnp.where(row_lane < rows, total, 1.0)
        scales.append([(shift / total).T for shift in shifts])
    gap = jnp.zeros((rows, LANES - cols), F32)
    expos = [[logit_buf[half, src].astype(F32).reshape(rows, heads * cols) for src in range(C)]
             for half in range(ratio)]
    span = groups * LANES
    for h in range(heads):
        weights = jnp.concatenate([
            jnp.concatenate([
                piece for src in range(C) for piece in (
                    expos[half][src][:, h * cols:(h + 1) * cols]
                    * scales[half][src][:rows, h:h + 1], gap)], axis=1)
            for half in range(ratio)], axis=0).astype(BF16)
        mean = jnp.dot(weights, values[:, h * span:(h + 1) * span], preferred_element_type=F32)
        mixed = (gates[:, h * span:(h + 1) * span] * mean).astype(BF16)
        for g in range(groups):
            at = (g * heads + h) * LANES
            gated[:, at:at + LANES] = mixed[:, g * LANES:(g + 1) * LANES]
    for g in range(groups):
        part = lax.dot_general(
            gated[:, g * heads * LANES:(g + 1) * heads * LANES], final_w_ref[...],
            (((1,), (1,)), ((), ())), preferred_element_type=F32)
        sl = slice(g * pack, (g + 1) * pack)
        msa_ref[sl] = (
            homolog_ref[sl].astype(F32) + part.T.reshape(pack, feats, cols)).astype(BF16)

    for t in range(1, R):
        right_copy(t).wait_send()
    for t in range(1, C):
        norm_copy(t).wait_send()
    for h in range(ratio):
        for t in range(C):
            @pl.when(jnp.logical_not((c * ratio + h == r) & (t == 0)))
            def _():
                left_copy(h, t).wait_send()

    def finish(k, carry):
        for t in range(1, R):
            logit_copy(k, t).wait_send()

        @pl.when(home != c)
        def _():
            logit_copy(k, 0).wait_send()

        return carry

    for t in range(1, R):
        stat_copy(t).wait_send()

    @pl.when(home != c)
    def _():
        stat_copy(0).wait_send()

    lax.fori_loop(0, chunks, finish, 0)


def local(
    R,
    C,
    homolog_matrix,
    contact_matrix,
    genuine_homolog_total,
    genuine_chain_length,
    tensor_product_matrices,
    tensor_product_final,
    mixing_value_gate_matrix,
    mixing_logit_matrix,
    mixing_final_matrix,
    feedforward_gate_expand,
    feedforward_shrink_matrix,
):
    seqs, cols, feats = homolog_matrix.shape
    rows, _, pair_width = contact_matrix.shape
    ch = tensor_product_matrices.shape[2] // 2
    heads = mixing_logit_matrix.shape[2]
    hidden = mixing_final_matrix.shape[1]
    head_width = hidden // heads
    ratio = R // C
    chunks = rows // 8
    pack = LANES // head_width
    groups = seqs // pack
    flipped = homolog_matrix.transpose(0, 2, 1)
    dims = (R, C, ratio, rows, cols, seqs * feats, heads, chunks)
    vmem = pl.BlockSpec(memory_space=pltpu.VMEM)
    smem = pl.BlockSpec(memory_space=pltpu.SMEM)
    dma = pltpu.SemaphoreType.DMA
    msa, pair_out = pl.pallas_call(
        functools.partial(kernel, dims),
        out_shape=(
            jax.ShapeDtypeStruct(flipped.shape, BF16),
            jax.ShapeDtypeStruct(contact_matrix.shape, BF16),
        ),
        in_specs=[smem] * 2 + [vmem] * 9,
        out_specs=(vmem, vmem),
        scratch_shapes=[
            pltpu.VMEM((R, seqs, ch * cols), BF16),
            pltpu.VMEM((R, seqs, rows * ch), BF16),
            pltpu.VMEM((C, cols, seqs * feats), BF16),
            pltpu.VMEM((chunks, 8, heads * cols), BF16),
            pltpu.VMEM((ratio, C, chunks, 8, heads * cols), BF16),
            pltpu.VMEM((2, heads, LANES), F32),
            pltpu.VMEM((ratio, C, 2, heads, LANES), F32),
            pltpu.VMEM((heads, 8, LANES), F32),
            pltpu.VMEM((R * seqs, ch * LANES), BF16),
            pltpu.VMEM((rows * ch, R * seqs), BF16),
            pltpu.VMEM((8, ch * ch, LANES), BF16),
            pltpu.VMEM((rows, cols, pair_width), BF16),
            pltpu.VMEM((rows, cols, pair_width), BF16),
            pltpu.VMEM((C * LANES, heads * groups * LANES), BF16),
            pltpu.VMEM((cols, heads * groups * LANES), F32),
            pltpu.VMEM((cols, heads * groups * LANES), BF16),
            pltpu.VMEM((pack * feats, heads * LANES), BF16),
            pltpu.VMEM((pack * feats, heads * LANES), BF16),
            pltpu.VMEM((pack * feats, heads * LANES), BF16),
            pltpu.VMEM((seqs, ch * cols), BF16),
            pltpu.VMEM((ratio, seqs, rows * ch), BF16),
            pltpu.VMEM((cols, seqs * feats), BF16),
            pltpu.VMEM((seqs * ch, LANES), F32),
            pltpu.VMEM((seqs * cols, LANES), F32),
            pltpu.VMEM((pair_width, ch * ch), BF16),
            pltpu.VMEM((ch * ch, pair_width), F32),
            dma((R,)), dma((R,)), dma((ratio, C)), dma((R,)), dma((C,)), dma((C,)),
            dma((chunks, R)), dma((ratio, C, chunks)), dma((R,)), dma((ratio, C)),
        ],
        compiler_params=pltpu.CompilerParams(
            collective_id=0, has_side_effects=True, vmem_limit_bytes=60 * 1024 * 1024
        ),
        name="msa_block",
    )(
        genuine_homolog_total, genuine_chain_length,
        flipped, contact_matrix, tensor_product_matrices[0],
        tensor_product_final[0], mixing_value_gate_matrix[0], mixing_logit_matrix[0].T, mixing_final_matrix[0].T,
        feedforward_gate_expand[0], feedforward_shrink_matrix[0],
    )
    return (msa.transpose(0, 2, 1), pair_out)


def solution(mesh):
    in_specs = (P("row", "col", None), P("row", "col", None)) + (P(),) * 9
    out_specs = (P("row", "col", None), P("row", "col", None))
    body = functools.partial(local, mesh.shape["row"], mesh.shape["col"])
    return jax.shard_map(body, mesh=mesh, in_specs=in_specs, out_specs=out_specs, check_vma=False)
```
